256 devices in a mesh: tm: 32 (over x, y, z_hi), span: 8 (over z_lo, core).
Axes of the slice: x: 4, y: 4, z: 8 (z_hi: 2, z_lo: 4; z = z_hi * 4 + z_lo), core: 2. Of those that a mesh axis runs over, the one named last changes fastest.
Arguments:
- frames: bfloat16 [32, 64, 256, 128], P('tm', None, 'span'), may hold values from -6 to 6
- cotangent: bfloat16 [32, 64, 256, 128], P('tm', None, 'span'), may hold values from -6 to 6
- spatial_weight: bfloat16 [3, 3, 64, 64], replicated, may hold values from -0.25 to 0.25
- temporal_kernel: bfloat16 [64, 32], replicated, may hold values from -1 to 1
Outputs:
- block_output: bfloat16 [32, 64, 256, 128], P('tm', None, 'span')
- input_grad: bfloat16 [32, 64, 256, 128], P('tm', None, 'span')
- weight_grad: float32 [3, 3, 64, 64], replicated
- kernel_grad: float32 [64, 32], replicated
The draws below stay inside these ranges and needn't reach their ends.
All inputs are finite; a program needn't handle non-finite values.
Results may differ from the reference program's by a relative error of at most 0.0051.
Values may be sent and summed in bfloat16 or wider, within the bound.
A program may use at most 64 MiB of HBM per device.

```python
import jax
import jax.numpy as jnp
from jax import lax

C = 64
CW = 128
TF = 32
SP = 256


def block_scale(key, dims, pieces, smallest, largest):
    def one(position, shards_of):
        heights = jax.random.uniform(jax.random.fold_in(jax.random.fold_in(key, 6), position), (shards_of,), jnp.float32, smallest / len(pieces), largest / len(pieces))
        return jnp.repeat(jnp.exp(heights), dims[position] // shards_of).reshape((-1,) + (1,) * (len(dims) - position - 1))

    level = one(*pieces[0])
    for cut in pieces[1:]:
        level = level * one(*cut)
    return level


def centred(stream_key, extent, spread, limit, pieces=(), kind=jnp.bfloat16):
    entries = jax.random.normal(stream_key, extent, jnp.float32) * spread
    if len(pieces) > 0:
        entries = block_scale(stream_key, extent, pieces, -0.22, 0.18) * entries
    return jnp.clip(entries, min=-limit, max=limit).astype(kind)


def setup_inputs(seed: int = 0) -> dict:
    arg_keys = jax.random.split(jax.random.key(seed), 5)
    frames = centred(arg_keys[0], (TF, C, SP, CW), 1.0, 6.0, ((0, 32), (2, 8)))
    cotangent = centred(arg_keys[1], (TF, C, SP, CW), 1.0, 6.0, ((0, 32), (2, 8)))
    spatial_weight = centred(arg_keys[2], (3, 3, C, C), (9 * C) ** -0.5, 0.25)
    temporal_kernel = centred(arg_keys[3], (C, TF), TF ** -0.5, 1.0)
    return dict(frames=frames, cotangent=cotangent, spatial_weight=spatial_weight, temporal_kernel=temporal_kernel)


def toeplitz(kernel):
    count = kernel.shape[1]
    chans = kernel.shape[0]
    vector = jnp.concatenate([jnp.zeros((chans, 1), kernel.dtype), kernel[:, ::-1], jnp.zeros((chans, count - 1), kernel.dtype)], axis=1)
    tiled = jnp.tile(vector, (1, count))
    skewed = tiled[:, count:count + count * (2 * count - 1)].reshape(chans, count, 2 * count - 1)
    return skewed[:, :, :count]


def diagonal_sums(products):
    chans = products.shape[0]
    count = products.shape[1]
    flipped = products[:, :, ::-1]
    wide = jnp.concatenate([flipped, jnp.zeros_like(flipped)], axis=2)
    skewed = wide.reshape(chans, 2 * count * count)[:, :count * (2 * count - 1)].reshape(chans, count, 2 * count - 1)
    return jnp.sum(skewed[:, :, count - 1:], axis=1)


def convolve(field, weights):
    return lax.conv_general_dilated(field[None], weights, (1, 1), ((1, 1), (1, 1)), dimension_numbers=("NCHW", "OIHW", "NCHW"))[0]


def reference(frames, cotangent, spatial_weight, temporal_kernel):
    forward_w = spatial_weight.astype(jnp.float32).transpose(2, 3, 0, 1)
    flipped_w = spatial_weight.astype(jnp.float32)[::-1, ::-1].transpose(3, 2, 0, 1)
    gscale = float(TF * SP * CW) ** -0.5

    def activate(frame):
        hidden = convolve(frame.astype(jnp.float32), forward_w)
        return (hidden * jax.nn.sigmoid(hidden)).astype(jnp.bfloat16)

    active = lax.map(activate, frames)
    toe = toeplitz(temporal_kernel).astype(jnp.float32)
    flat_act = active.reshape(TF, C, SP * CW).astype(jnp.float32)
    flat_cot = cotangent.reshape(TF, C, SP * CW).astype(jnp.float32)
    along = jnp.einsum("cts,scn->tcn", toe, flat_act).astype(jnp.bfloat16)
    block_output = (frames.astype(jnp.float32) + along.reshape(frames.shape).astype(jnp.float32)).astype(jnp.bfloat16)
    back = jnp.einsum("cts,tcn->scn", toe, flat_cot).astype(jnp.bfloat16).reshape(frames.shape)
    kernel_grad = diagonal_sums(jnp.einsum("tcn,scn->cts", flat_cot, flat_act)) * gscale

    def backward(carry, inputs):
        frame, cot_frame, back_frame = inputs
        field = frame.astype(jnp.float32)
        hidden = convolve(field, forward_w)
        sigma = jax.nn.sigmoid(hidden)
        dhidden = (back_frame.astype(jnp.float32) * sigma * (1.0 + hidden * (1.0 - sigma))).astype(jnp.bfloat16)
        dfield = dhidden.astype(jnp.float32)
        grad_frame = (cot_frame.astype(jnp.float32) + convolve(dfield, flipped_w)).astype(jnp.bfloat16)
        padded = jnp.pad(field, ((0, 0), (1, 1), (1, 1)))
        terms = jnp.stack([jnp.einsum("osw,isw->oi", dfield, padded[:, row_off:row_off + SP, col_off:col_off + CW]) for row_off in range(3) for col_off in range(3)]).reshape(3, 3, C, C)
        return carry + terms, grad_frame

    weight_sum, input_grad = lax.scan(backward, jnp.zeros((3, 3, C, C), jnp.float32), (frames, cotangent, back))
    return block_output, input_grad, weight_sum * gscale, kernel_grad
```

```python
import functools

import jax
import jax.numpy as jnp
from jax import lax
from jax.experimental import pallas as pl
from jax.experimental.pallas import tpu as pltpu
from jax.sharding import PartitionSpec as P

F32 = jnp.float32
BF16 = jnp.bfloat16
MESH = pl.DeviceIdType.MESH
LANES = 128
BLK = 8


def causal_sums(n, x_at, k_at, put):
    for tb in range(0, n, BLK):
        acc = [None] * BLK
        for rb in range(0, tb + BLK, BLK):
            xs = [x_at(rb + j) for j in range(BLK)]
            ks = {}
            for lag in range(max(0, tb - rb - BLK + 1), tb - rb + BLK):
                ks[lag] = k_at(lag)
            for i in range(BLK):
                for j in range(BLK):
                    lag = tb + i - rb - j
                    if lag >= 0:
                        term = ks[lag] * xs[j]
                        acc[i] = term if acc[i] is None else acc[i] + term
        for i in range(BLK):
            put(tb + i, acc[i])


def lag_sums(n, t_at, r_at, put):
    acc = {}
    for dist in range(0, n, BLK):
        for rb in range(0, n - dist, BLK):
            ts = [t_at(rb + dist + i) for i in range(BLK)]
            rs = [r_at(rb + j) for j in range(BLK)]
            for i in range(BLK):
                for j in range(BLK):
                    lag = dist + i - j
                    if lag >= 0:
                        term = ts[i] * rs[j]
                        acc[lag] = acc[lag] + term if lag in acc else term
        for lag in sorted(acc):
            if lag <= dist:
                put(lag, acc.pop(lag))
    for lag in sorted(acc):
        put(lag, acc.pop(lag))


def kernel(
    n,
    nspan,
    gscale,
    frames_ref,
    cot_ref,
    wf_ref,
    wb_ref,
    temporal_ref,
    block_ref,
    input_grad_ref,
    weight_grad_ref,
    kernel_grad_ref,
    tmp,
    xp,
    x3,
    cot_t,
    act_t,
    gbuf,
    kb,
    rcot,
    ract,
    xf,
    yf,
    outf,
    back_t,
    along_t,
    rback,
    ralong,
    dp,
    db,
    igf,
    kgbuf,
    red,
    rred,
    part,
    zpart,
    full,
    gathered,
    send_sems,
    recv_sems,
):
    me = lax.axis_index("tm")
    sp = lax.axis_index("span")
    xy, zh = me // 2, me % 2
    zl, core = sp // 2, sp % 2
    zcount = nspan
    zi = zh * (nspan // 2) + zl
    pi = xy * 2 + core
    ch = 64

    def tm_dev(t):
        return (t, sp)

    def plane_dev(p):
        return ((p // 2) * 2 + zh, zl * 2 + p % 2)

    def z_dev(z):
        return (xy * 2 + z // (nspan // 2), (z % (nspan // 2)) * 2 + core)

    barrier = pltpu.get_barrier_semaphore()

    def greet(dev):
        pl.semaphore_signal(barrier, inc=1, device_id=dev, device_id_type=MESH)

    @pl.loop(1, n)
    def _(k):
        greet(tm_dev(lax.rem(me + k, n)))

    @pl.loop(0, n // 2)
    def _(k):
        greet(plane_dev(2 * lax.rem(xy + k, n // 2) + 1 - core))

    @pl.loop(1, zcount // 2)
    def _(k):
        greet(z_dev(lax.rem(zi + k, zcount)))
        greet(z_dev(lax.rem(zi + zcount - k, zcount)))

    greet((me, lax.rem(sp + 1, nspan)))
    greet((me, lax.rem(sp + nspan - 1, nspan)))

    lane = lax.broadcasted_iota(jnp.int32, (ch, LANES), 1)

    def right(v):
        return jnp.where(lane == 0, 0.0, pltpu.roll(v, 1, 1))

    def left(v):
        return jnp.where(lane == LANES - 1, 0.0, pltpu.roll(v, LANES - 1, 1))

    @pl.loop(0, ch)
    def _(c):
        tmp[pl.ds(c, n, stride=ch), :] = cot_ref[0, c].astype(F32)

    @pl.loop(0, n)
    def _(r):
        cot_t[r] = tmp[pl.ds(pl.multiple_of(r * ch, ch), ch), :].astype(BF16)

    @pl.loop(0, ch)
    def _(c):
        tmp[pl.ds(c, n, stride=ch), :] = frames_ref[0, c].astype(F32)

    @pl.loop(0, n)
    def _(r):
        xp[r + 1] = tmp[pl.ds(pl.multiple_of(r * ch, ch), ch), :].astype(BF16)

    @pl.when(sp == 0)
    def _():
        xp[0] = jnp.zeros((ch, LANES), BF16)
        dp[0] = jnp.zeros((ch, LANES), BF16)

    @pl.when(sp == nspan - 1)
    def _():
        xp[n + 1] = jnp.zeros((ch, LANES), BF16)
        dp[n + 1] = jnp.zeros((ch, LANES), BF16)

    def row_cols(s):
        return pl.ds(pl.multiple_of(s * LANES, LANES), LANES)

    def load_taps(s):
        for a in range(3):
            x3[a * ch : (a + 1) * ch, row_cols(s)] = xp[s + a]

    def forward_rows(rows):
        taps = jnp.concatenate([x3[:, row_cols(s)] for s in rows], axis=1)
        out = jnp.dot(wf_ref[...], taps, preferred_element_type=F32)
        for k, s in enumerate(rows):
            o = out[:, k * LANES : (k + 1) * LANES]
            hidden = o[ch : 2 * ch] + right(o[:ch]) + left(o[2 * ch :])
            sigma = jax.nn.sigmoid(hidden)
            act_t[s] = (hidden * sigma).astype(BF16)
            gbuf[s] = sigma * (1.0 + hidden * (1.0 - sigma))

    @pl.loop(1, n - 1)
    def _(s):
        load_taps(s)

    @pl.loop(0, (n - 2) // 2)
    def _(p):
        forward_rows([1 + 2 * p, 2 + 2 * p])

    pl.semaphore_wait(barrier, n - 1 + n // 2 + 2 * (zcount // 2 - 1) + 2)

    def exchange(src, dst, idx, k):
        peer = lax.rem(me + k, n)
        return pltpu.make_async_remote_copy(
            src_ref=src.at[peer],
            dst_ref=dst.at[me],
            send_sem=send_sems.at[idx],
            recv_sem=recv_sems.at[idx],
            device_id=tm_dev(peer),
            device_id_type=MESH,
        )

    def start_exchange(src, dst, idx):
        @pl.loop(0, n // 2)
        def _(k):
            exchange(src, dst, idx, 2 * k + 1).start()

        @pl.loop(1, n // 2)
        def _(k):
            exchange(src, dst, idx, 2 * k).start()

        dst[me] = src[me]

    def all_of(buf, count, idx):
        view = buf.at[pl.ds(0, count)]
        return pltpu.make_async_remote_copy(
            src_ref=view,
            dst_ref=view,
            send_sem=send_sems.at[idx],
            recv_sem=recv_sems.at[idx],
            device_id=tm_dev(lax.rem(me + 1, n)),
            device_id_type=MESH,
        )

    def halo(buf, idx):
        up = pltpu.make_async_remote_copy(
            src_ref=buf.at[n],
            dst_ref=buf.at[0],
            send_sem=send_sems.at[idx],
            recv_sem=recv_sems.at[idx],
            device_id=(me, sp + 1),
            device_id_type=MESH,
        )
        down = pltpu.make_async_remote_copy(
            src_ref=buf.at[1],
            dst_ref=buf.at[n + 1],
            send_sem=send_sems.at[idx + 1],
            recv_sem=recv_sems.at[idx + 1],
            device_id=(me, sp - 1),
            device_id_type=MESH,
        )
        return up, down

    def start_halo(buf, idx):
        up, down = halo(buf, idx)

        @pl.when(sp < nspan - 1)
        def _():
            up.start()

        @pl.when(sp > 0)
        def _():
            down.start()

    def finish_halo(buf, idx):
        up, down = halo(buf, idx)

        @pl.when(sp > 0)
        def _():
            up.wait_recv()

        @pl.when(sp < nspan - 1)
        def _():
            down.wait_recv()

        @pl.when(sp < nspan - 1)
        def _():
            up.wait_send()

        @pl.when(sp > 0)
        def _():
            down.wait_send()

    start_halo(xp, 0)
    start_exchange(cot_t, rcot, 4)
    finish_halo(xp, 0)
    load_taps(0)
    load_taps(n - 1)
    forward_rows([0, n - 1])
    start_exchange(act_t, ract, 5)

    for lag in range(n):
        kb[lag] = jnp.broadcast_to(temporal_ref[:, lag : lag + 1].astype(F32), (ch, LANES))

    def chan(c):
        return pl.ds(pl.multiple_of(c * 8, 8), 8)

    all_of(rcot, n - 1, 4).wait_recv()

    @pl.loop(0, n)
    def _(t):
        yf[t] = rcot[t].astype(F32)

    @pl.loop(0, ch // 8)
    def _(c):
        def put(t, v):
            outf[n - 1 - t, chan(c), :] = v

        causal_sums(n, lambda t: yf[n - 1 - t, chan(c), :], lambda lag: kb[lag, chan(c), :], put)

    @pl.loop(0, n)
    def _(t):
        back_t[t] = outf[t].astype(BF16)

    start_exchange(back_t, rback, 6)

    all_of(ract, n - 1, 5).wait_recv()

    @pl.loop(0, n)
    def _(t):
        xf[t] = ract[t].astype(F32)

    @pl.loop(0, ch // 8)
    def _(c):
        def put(t, v):
            outf[t, chan(c), :] = v

        causal_sums(n, lambda t: xf[t, chan(c), :], lambda lag: kb[lag, chan(c), :], put)

    @pl.loop(0, n)
    def _(t):
        along_t[t] = outf[t].astype(BF16)

    start_exchange(along_t, ralong, 7)

    lane8 = lax.broadcasted_iota(jnp.int32, (8, 2 * LANES), 1)

    @pl.loop(0, ch // 8)
    def _(c):
        total = [jnp.zeros((8, 2 * LANES), F32)]

        def put(lag, v):
            row = jnp.sum(v, axis=1, keepdims=True)
            total[0] = jnp.where(lane8 == lag, row, total[0])

        lag_sums(n, lambda t: yf[t, chan(c), :], lambda r: xf[r, chan(c), :], put)
        kgbuf[chan(c), :] = total[0]

    all_of(rback, n - 1, 6).wait_recv()

    def gate_row(s):
        v = rback[s].astype(F32) * gbuf[s]
        dp[s + 1] = v.astype(BF16)
        db[:ch, row_cols(s)] = left(v).astype(BF16)
        db[ch : 2 * ch, row_cols(s)] = v.astype(BF16)
        db[2 * ch :, row_cols(s)] = right(v).astype(BF16)

    gate_row(0)
    gate_row(n - 1)
    start_halo(dp, 2)

    @pl.loop(1, n - 1)
    def _(s):
        gate_row(s)

    grads = lax.dot_general(
        db[...], x3[...], (((1,), (1,)), ((), ())), preferred_element_type=F32
    )
    per = 192 // n
    kper = ch // n
    grads = jnp.concatenate([grads, jnp.zeros((192, 64), F32)], axis=1)
    for k in range(n):
        red[k, 0:per, :] = grads[k * per : (k + 1) * per]
        red[k, per : per + kper, :] = kgbuf[k * kper : (k + 1) * kper, :]

    def plane_copy(src, dst, idx, peer):
        return pltpu.make_async_remote_copy(
            src_ref=src,
            dst_ref=dst.at[pi],
            send_sem=send_sems.at[idx],
            recv_sem=recv_sems.at[idx],
            device_id=plane_dev(peer),
            device_id_type=MESH,
        )

    @pl.loop(1, n)
    def _(k):
        peer = lax.rem(pi + k, n)
        plane_copy(red.at[peer], rred, 8, peer).start()

    rred[pi] = red[pi]

    def backward_rows(rows):
        taps = jnp.concatenate(
            [jnp.concatenate([dp[s + j] for j in range(3)], axis=0) for s in rows], axis=1
        )
        out = jnp.dot(wb_ref[...], taps, preferred_element_type=F32)
        for k, s in enumerate(rows):
            o = out[:, k * LANES : (k + 1) * LANES]
            igf[pl.ds(pl.multiple_of(s * ch, ch), ch), :] = (
                o[ch : 2 * ch] + left(o[:ch]) + right(o[2 * ch :])
            )

    @pl.loop(0, (n - 2) // 2)
    def _(p):
        backward_rows([1 + 2 * p, 2 + 2 * p])

    all_of(rred, n - 1, 8).wait_recv()
    part[...] = jnp.sum(rred[...], axis=0)

    def z_copy(k):
        peer = lax.rem(zi + k, zcount)
        return pltpu.make_async_remote_copy(
            src_ref=part,
            dst_ref=zpart.at[zi],
            send_sem=send_sems.at[9],
            recv_sem=recv_sems.at[9],
            device_id=z_dev(peer),
            device_id_type=MESH,
        )

    @pl.loop(1, zcount)
    def _(k):
        z_copy(k).start()

    zpart[zi] = part[...]

    finish_halo(dp, 2)
    backward_rows([0, n - 1])

    all_of(zpart, zcount - 1, 9).wait_recv()
    full[...] = jnp.sum(zpart[...], axis=0) * gscale

    @pl.loop(1, n)
    def _(k):
        peer = lax.rem(pi + k, n)
        plane_copy(full, gathered, 10, peer).start()

    gathered[pi] = full[...]

    @pl.loop(0, ch)
    def _(c):
        input_grad_ref[0, c] = (
            cot_ref[0, c].astype(F32) + igf[pl.ds(c, n, stride=ch), :]
        ).astype(BF16)

    all_of(ralong, n - 1, 7).wait_recv()

    @pl.loop(0, n)
    def _(r):
        tmp[pl.ds(pl.multiple_of(r * ch, ch), ch), :] = ralong[r].astype(F32)

    @pl.loop(0, ch)
    def _(c):
        block_ref[0, c] = (
            frames_ref[0, c].astype(F32) + tmp[pl.ds(c, n, stride=ch), :]
        ).astype(BF16)

    all_of(gathered, n - 1, 10).wait_recv()
    whole = jnp.concatenate([gathered[k, 0:per, :] for k in range(n)], axis=0)
    for a in range(3):
        for b in range(3):
            weight_grad_ref[a, b] = whole[b * ch : (b + 1) * ch, a * ch : (a + 1) * ch]
    kernel_grad_ref[...] = jnp.concatenate(
        [gathered[k, per : per + kper, 0:n] for k in range(n)], axis=0
    )

    all_of(rcot, n - 1, 4).wait_send()
    all_of(ract, n - 1, 5).wait_send()
    all_of(rback, n - 1, 6).wait_send()
    all_of(ralong, n - 1, 7).wait_send()
    all_of(rred, n - 1, 8).wait_send()
    all_of(zpart, zcount - 1, 9).wait_send()
    all_of(gathered, n - 1, 10).wait_send()


def local(frames, cotangent, spatial_weight, temporal_kernel):
    n = lax.axis_size("tm")
    nspan = lax.axis_size("span")
    _, ch, rows, width = frames.shape
    assert rows == n and ch == 64 and width == LANES and frames.shape[0] == 1
    gscale = float(n * rows * nspan * width) ** (-0.5)
    wf = spatial_weight.transpose(1, 2, 0, 3).reshape(3 * ch, 3 * ch)
    wb = spatial_weight[::-1].transpose(1, 3, 0, 2).reshape(3 * ch, 3 * ch)
    block = (n, ch, LANES)
    red = (n, 256 // n, 256)

    def vmem(shape, dtype):
        return pltpu.VMEM(shape, dtype)

    spec = pl.BlockSpec(memory_space=pltpu.VMEM)
    return pl.pallas_call(
        functools.partial(kernel, n, nspan, gscale),
        name="space_time_block",
        out_shape=(
            jax.ShapeDtypeStruct(frames.shape, BF16),
            jax.ShapeDtypeStruct(frames.shape, BF16),
            jax.ShapeDtypeStruct((3, 3, ch, ch), F32),
            jax.ShapeDtypeStruct((ch, n), F32),
        ),
        in_specs=[spec] * 5,
        out_specs=(spec,) * 4,
        scratch_shapes=[
            vmem((n * ch, LANES), F32),
            vmem((n + 2, ch, LANES), BF16),
            vmem((3 * ch, n * LANES), BF16),
            vmem(block, BF16),
            vmem(block, BF16),
            vmem(block, F32),
            vmem(block, F32),
            vmem(block, BF16),
            vmem(block, BF16),
            vmem(block, F32),
            vmem(block, F32),
            vmem(block, F32),
            vmem(block, BF16),
            vmem(block, BF16),
            vmem(block, BF16),
            vmem(block, BF16),
            vmem((n + 2, ch, LANES), BF16),
            vmem((3 * ch, n * LANES), BF16),
            vmem((n * ch, LANES), F32),
            vmem((ch, 256), F32),
            vmem(red, F32),
            vmem(red, F32),
            vmem(red[1:], F32),
            vmem((nspan,) + red[1:], F32),
            vmem(red[1:], F32),
            vmem(red, F32),
            pltpu.SemaphoreType.DMA((11,)),
            pltpu.SemaphoreType.DMA((11,)),
        ],
        compiler_params=pltpu.CompilerParams(
            collective_id=0, has_side_effects=True, vmem_limit_bytes=48 * 2**20
        ),
    )(frames, cotangent, wf, wb, temporal_kernel)


def solution(mesh):
    placed = (P("tm", None, "span", None), P("tm", None, "span", None), P(), P())
    return jax.shard_map(
        local,
        mesh=mesh,
        in_specs=placed,
        out_specs=placed,
        check_vma=False,
    )
```

```python
import functools

import jax
import jax.numpy as jnp
from jax import lax
from jax.experimental import pallas as pl
from jax.experimental.pallas import tpu as pltpu
from jax.sharding import PartitionSpec as P

F32 = jnp.float32
BF16 = jnp.bfloat16
MESH = pl.DeviceIdType.MESH
LANES = 128
BLK = 8


def causal_sums(n, x_at, k_at, put):
    for tb in range(0, n, BLK):
        acc = [None] * BLK
        for rb in range(0, tb + BLK, BLK):
            xs = [x_at(rb + j) for j in range(BLK)]
            ks = {}
            for lag in range(max(0, tb - rb - BLK + 1), tb - rb + BLK):
                ks[lag] = k_at(lag)
            for i in range(BLK):
                for j in range(BLK):
                    lag = tb + i - rb - j
                    if lag >= 0:
                        term = ks[lag] * xs[j]
                        acc[i] = term if acc[i] is None else acc[i] + term
        for i in range(BLK):
            put(tb + i, acc[i])


def lag_sums(n, t_at, r_at, put):
    acc = {}
    for dist in range(0, n, BLK):
        for rb in range(0, n - dist, BLK):
            ts = [t_at(rb + dist + i) for i in range(BLK)]
            rs = [r_at(rb + j) for j in range(BLK)]
            for i in range(BLK):
                for j in range(BLK):
                    lag = dist + i - j
                    if lag >= 0:
                        term = ts[i] * rs[j]
                        acc[lag] = acc[lag] + term if lag in acc else term
        for lag in sorted(acc):
            if lag <= dist:
                put(lag, acc.pop(lag))
    for lag in sorted(acc):
        put(lag, acc.pop(lag))


def kernel(
    n,
    nspan,
    gscale,
    frames_hbm,
    cot_hbm,
    weight_hbm,
    temporal_hbm,
    block_ref,
    input_grad_ref,
    weight_grad_ref,
    kernel_grad_ref,
    frames_ref,
    cot_ref,
    weight_ref,
    temporal_ref,
    tmp,
    wf,
    wb,
    xp,
    x3,
    cot_t,
    act_t,
    gbuf,
    kb,
    rcot,
    ract,
    xf,
    yf,
    outf,
    back_t,
    along_t,
    rback,
    ralong,
    dp,
    db,
    igf,
    kgbuf,
    kz,
    kp,
    red,
    rred,
    part,
    zpart,
    full,
    gathered,
    send_sems,
    recv_sems,
    load_sems,
):
    me = lax.axis_index("tm")
    sp = lax.axis_index("span")
    xy, zh = me // 2, me % 2
    zl, core = sp // 2, sp % 2
    zcount = nspan
    zi = zh * (nspan // 2) + zl
    pi = xy * 2 + core
    ch = 64

    def tm_dev(t):
        return (t, sp)

    def plane_dev(p):
        return ((p // 2) * 2 + zh, zl * 2 + p % 2)

    def z_dev(z):
        return (xy * 2 + z // (nspan // 2), (z % (nspan // 2)) * 2 + core)

    loads = [
        pltpu.make_async_copy(src, dst, load_sems.at[k])
        for k, (src, dst) in enumerate(
            [
                (cot_hbm, cot_ref),
                (frames_hbm, frames_ref),
                (weight_hbm, weight_ref),
                (temporal_hbm, temporal_ref),
            ]
        )
    ]
    for load in loads:
        load.start()

    barrier = pltpu.get_barrier_semaphore()

    def greet(dev):
        pl.semaphore_signal(barrier, inc=1, device_id=dev, device_id_type=MESH)

    @pl.loop(1, n)
    def _(k):
        greet(tm_dev(lax.rem(me + k, n)))

    @pl.loop(0, n // 2)
    def _(k):
        greet(plane_dev(2 * lax.rem(xy + k, n // 2) + 1 - core))

    @pl.loop(1, zcount // 2)
    def _(k):
        greet(z_dev(lax.rem(zi + k, zcount)))
        greet(z_dev(lax.rem(zi + zcount - k, zcount)))

    greet((me, lax.rem(sp + 1, nspan)))
    greet((me, lax.rem(sp + nspan - 1, nspan)))

    lane = lax.broadcasted_iota(jnp.int32, (ch, LANES), 1)

    def right(v):
        return jnp.where(lane == 0, 0.0, pltpu.roll(v, 1, 1))

    def left(v):
        return jnp.where(lane == LANES - 1, 0.0, pltpu.roll(v, LANES - 1, 1))

    def rows_first(src, dst, offset):
        @pl.loop(0, ch, unroll=8)
        def _(c):
            tmp[pl.ds(c, n, stride=ch), :] = src[0, c].astype(F32)

        @pl.loop(0, n, unroll=4)
        def _(r):
            dst[r + offset] = tmp[pl.ds(pl.multiple_of(r * ch, ch), ch), :].astype(BF16)

    loads[0].wait()
    rows_first(cot_ref, cot_t, 0)
    loads[1].wait()
    rows_first(frames_ref, xp, 1)
    loads[2].wait()
    loads[3].wait()

    wide = []
    for b in range(3):
        wide.append(jnp.concatenate([weight_ref[a, b].astype(F32) for a in range(3)], axis=1))
    wf[...] = jnp.concatenate(wide, axis=0).astype(BF16)
    wide = []
    for j in range(3):
        wide.append(jnp.concatenate([weight_ref[2 - j, b].astype(F32) for b in range(3)], axis=1))
    wb[...] = jnp.concatenate(wide, axis=0).T.astype(BF16)

    @pl.when(sp == 0)
    def _():
        xp[0] = jnp.zeros((ch, LANES), BF16)
        dp[0] = jnp.zeros((ch, LANES), BF16)

    @pl.when(sp == nspan - 1)
    def _():
        xp[n + 1] = jnp.zeros((ch, LANES), BF16)
        dp[n + 1] = jnp.zeros((ch, LANES), BF16)

    def row_cols(s):
        return pl.ds(pl.multiple_of(s * LANES, LANES), LANES)

    def load_taps(s):
        for a in range(3):
            x3[a * ch : (a + 1) * ch, row_cols(s)] = xp[s + a]

    def forward_rows(rows):
        taps = jnp.concatenate([x3[:, row_cols(s)] for s in rows], axis=1)
        out = jnp.dot(wf[...], taps, preferred_element_type=F32)
        for k, s in enumerate(rows):
            o = out[:, k * LANES : (k + 1) * LANES]
            hidden = o[ch : 2 * ch] + right(o[:ch]) + left(o[2 * ch :])
            sigma = jax.nn.sigmoid(hidden)
            act_t[s] = (hidden * sigma).astype(BF16)
            gbuf[s] = sigma * (1.0 + hidden * (1.0 - sigma))

    @pl.loop(1, n - 1, unroll=2)
    def _(s):
        load_taps(s)

    pl.semaphore_wait(barrier, n - 1 + n // 2 + 2 * (zcount // 2 - 1) + 2)

    def exchange(src, dst, idx, k, lo, size):
        peer = lax.rem(me + k, n)
        return pltpu.make_async_remote_copy(
            src_ref=src.at[peer, pl.ds(lo, size)],
            dst_ref=dst.at[me, pl.ds(lo, size)],
            send_sem=send_sems.at[idx],
            recv_sem=recv_sems.at[idx],
            device_id=tm_dev(peer),
            device_id_type=MESH,
        )

    def start_exchange(src, dst, idx, lo=0, size=64):
        @pl.loop(0, n // 2)
        def _(k):
            exchange(src, dst, idx, 2 * k + 1, lo, size).start()

        @pl.loop(1, n // 2)
        def _(k):
            exchange(src, dst, idx, 2 * k, lo, size).start()

        dst[me, lo : lo + size] = src[me, lo : lo + size]

    def all_of(buf, idx, lo=0, size=64):
        view = buf.at[pl.ds(0, n - 1), pl.ds(lo, size)]
        return pltpu.make_async_remote_copy(
            src_ref=view,
            dst_ref=view,
            send_sem=send_sems.at[idx],
            recv_sem=recv_sems.at[idx],
            device_id=tm_dev(lax.rem(me + 1, n)),
            device_id_type=MESH,
        )

    def halo(buf, idx):
        up = pltpu.make_async_remote_copy(
            src_ref=buf.at[n],
            dst_ref=buf.at[0],
            send_sem=send_sems.at[idx],
            recv_sem=recv_sems.at[idx],
            device_id=(me, sp + 1),
            device_id_type=MESH,
        )
        down = pltpu.make_async_remote_copy(
            src_ref=buf.at[1],
            dst_ref=buf.at[n + 1],
            send_sem=send_sems.at[idx + 1],
            recv_sem=recv_sems.at[idx + 1],
            device_id=(me, sp - 1),
            device_id_type=MESH,
        )
        return up, down

    def start_halo(buf, idx):
        up, down = halo(buf, idx)

        @pl.when(sp < nspan - 1)
        def _():
            up.start()

        @pl.when(sp > 0)
        def _():
            down.start()

    def finish_halo(buf, idx):
        up, down = halo(buf, idx)

        @pl.when(sp > 0)
        def _():
            up.wait_recv()

        @pl.when(sp < nspan - 1)
        def _():
            down.wait_recv()

        @pl.when(sp < nspan - 1)
        def _():
            up.wait_send()

        @pl.when(sp > 0)
        def _():
            down.wait_send()

    start_halo(xp, 0)
    start_exchange(cot_t, rcot, 4)

    @pl.loop(0, (n - 2) // 2, unroll=3)
    def _(p):
        forward_rows([1 + 2 * p, 2 + 2 * p])

    finish_halo(xp, 0)
    load_taps(0)
    load_taps(n - 1)
    forward_rows([0, n - 1])
    half = ch // 2
    start_exchange(act_t, ract, 5, 0, half)

    columns = temporal_ref[...].astype(F32).T
    for lag in range(n):
        kb[lag] = jnp.broadcast_to(columns[:, lag : lag + 1], (ch, LANES))

    def chan(c):
        return pl.ds(pl.multiple_of(c * 8, 8), 8)

    all_of(rcot, 4).wait_recv()

    @pl.loop(0, n, unroll=4)
    def _(t):
        yf[t] = rcot[t].astype(F32)

    @pl.loop(0, ch // 8)
    def _(c):
        def put(t, v):
            outf[n - 1 - t, chan(c), :] = v

        causal_sums(n, lambda t: yf[n - 1 - t, chan(c), :], lambda lag: kb[lag, chan(c), :], put)

    @pl.loop(0, n, unroll=4)
    def _(t):
        back_t[t] = outf[t].astype(BF16)

    start_exchange(back_t, rback, 6)
    start_exchange(act_t, ract, 11, half, half)

    lane8 = lax.broadcasted_iota(jnp.int32, (8, LANES), 1)

    def along_half(h, in_idx, out_idx):
        lo = h * half
        all_of(ract, in_idx, lo, half).wait_recv()

        @pl.loop(0, n, unroll=4)
        def _(t):
            xf[t, lo : lo + half] = ract[t, lo : lo + half].astype(F32)

        @pl.loop(h * (half // 8), (h + 1) * (half // 8))
        def _(c):
            def put(t, v):
                outf[t, chan(c), :] = v

            causal_sums(n, lambda t: xf[t, chan(c), :], lambda lag: kb[lag, chan(c), :], put)

        @pl.loop(0, n, unroll=4)
        def _(t):
            along_t[t, lo : lo + half] = outf[t, lo : lo + half].astype(BF16)

        start_exchange(along_t, ralong, out_idx, lo, half)

        @pl.loop(h * (half // 8), (h + 1) * (half // 8))
        def _(c):
            total = [jnp.zeros((8, LANES), F32)]

            def put(lag, v):
                row = jnp.sum(v, axis=1, keepdims=True)
                total[0] = jnp.where(lane8 == lag, row, total[0])

            lag_sums(n, lambda t: yf[t, chan(c), :], lambda r: xf[r, chan(c), :], put)
            kgbuf[chan(c), :] = total[0]

    along_half(0, 5, 7)

    all_of(rback, 6).wait_recv()

    def gate_row(s):
        v = rback[s].astype(F32) * gbuf[s]
        dp[s + 1] = v.astype(BF16)
        db[:ch, row_cols(s)] = left(v).astype(BF16)
        db[ch : 2 * ch, row_cols(s)] = v.astype(BF16)
        db[2 * ch :, row_cols(s)] = right(v).astype(BF16)

    gate_row(0)
    gate_row(n - 1)
    start_halo(dp, 2)

    @pl.loop(1, n - 1, unroll=5 if (n - 2) % 5 == 0 else 2)
    def _(s):
        gate_row(s)

    grads = lax.dot_general(
        db[...], x3[...], (((1,), (1,)), ((), ())), preferred_element_type=F32
    )
    per = 32 // n
    used = 9 * per
    pad = (used + 7) // 8 * 8
    for a in range(3):
        for b in range(3):
            tap = grads[b * ch : (b + 1) * ch, a * ch : (a + 1) * ch]
            tap = jnp.concatenate([tap[: ch // 2], tap[ch // 2 :]], axis=1)
            for j in range(per):
                at = (a * 3 + b) * per + j
                red[pl.ds(at, n, stride=pad), :] = tap[j * n : (j + 1) * n]

    def chunk(buf, k):
        return buf.at[pl.ds(pl.multiple_of(k * pad, pad), used)]

    def plane_copy(src, dst, idx, peer):
        return pltpu.make_async_remote_copy(
            src_ref=src,
            dst_ref=dst,
            send_sem=send_sems.at[idx],
            recv_sem=recv_sems.at[idx],
            device_id=plane_dev(peer),
            device_id_type=MESH,
        )

    @pl.loop(1, n)
    def _(k):
        peer = lax.rem(pi + k, n)
        plane_copy(chunk(red, peer), rred.at[pi, pl.ds(0, used)], 8, peer).start()

    rred[pi, 0:used, :] = red[pl.ds(pl.multiple_of(pi * pad, pad), used), :]

    def backward_rows(rows):
        taps = jnp.concatenate(
            [jnp.concatenate([dp[s + j] for j in range(3)], axis=0) for s in rows], axis=1
        )
        out = jnp.dot(wb[...], taps, preferred_element_type=F32)
        for k, s in enumerate(rows):
            o = out[:, k * LANES : (k + 1) * LANES]
            igf[pl.ds(pl.multiple_of(s * ch, ch), ch), :] = (
                o[ch : 2 * ch] + left(o[:ch]) + right(o[2 * ch :])
            )

    @pl.loop(0, (n - 2) // 2, unroll=3)
    def _(p):
        backward_rows([1 + 2 * p, 2 + 2 * p])

    along_half(1, 11, 12)
    lags = kgbuf[...].T[:n]
    kz[zi] = jnp.concatenate([lags[: n // 2], lags[n // 2 :]], axis=1)

    def lag_z(k):
        return pltpu.make_async_remote_copy(
            src_ref=kz.at[zi],
            dst_ref=kz.at[zi],
            send_sem=send_sems.at[13],
            recv_sem=recv_sems.at[13],
            device_id=z_dev(lax.rem(zi + k, zcount)),
            device_id_type=MESH,
        )

    @pl.loop(1, zcount)
    def _(k):
        lag_z(k).start()

    def many(buf, count, idx):
        view = buf.at[pl.ds(0, count)]
        return plane_copy(view, view, idx, lax.rem(pi + 1, n))

    def all_chunks(buf, count, idx):
        view = buf.at[pl.ds(0, count), pl.ds(0, used)]
        return plane_copy(view, view, idx, lax.rem(pi + 1, n))

    all_chunks(rred, n - 1, 8).wait_recv()
    part[0:used, :] = jnp.sum(rred[:, 0:used, :], axis=0)

    @pl.loop(1, zcount)
    def _(k):
        pltpu.make_async_remote_copy(
            src_ref=part.at[pl.ds(0, used)],
            dst_ref=zpart.at[zi, pl.ds(0, used)],
            send_sem=send_sems.at[9],
            recv_sem=recv_sems.at[9],
            device_id=z_dev(lax.rem(zi + k, zcount)),
            device_id_type=MESH,
        ).start()

    zpart[zi, 0:used, :] = part[0:used, :]

    many(kz, zcount - 1, 13).wait_recv()
    kp[pi] = jnp.sum(kz[...], axis=0) * gscale

    @pl.loop(1, n)
    def _(k):
        plane_copy(kp.at[pi], kp.at[pi], 14, lax.rem(pi + k, n)).start()

    finish_halo(dp, 2)
    backward_rows([0, n - 1])

    all_chunks(zpart, zcount - 1, 9).wait_recv()
    full[0:used, :] = jnp.sum(zpart[:, 0:used, :], axis=0) * gscale

    @pl.loop(1, n)
    def _(k):
        peer = lax.rem(pi + k, n)
        plane_copy(full.at[pl.ds(0, used)], chunk(gathered, pi), 10, peer).start()

    gathered[pl.ds(pl.multiple_of(pi * pad, pad), used), :] = full[0:used, :]

    @pl.loop(0, ch, unroll=8)
    def _(c):
        input_grad_ref[0, c] = (
            cot_ref[0, c].astype(F32) + igf[pl.ds(c, n, stride=ch), :]
        ).astype(BF16)

    all_of(ralong, 7, 0, half).wait_recv()
    all_of(ralong, 12, half, half).wait_recv()

    @pl.loop(0, n, unroll=4)
    def _(r):
        tmp[pl.ds(pl.multiple_of(r * ch, ch), ch), :] = ralong[r].astype(F32)

    @pl.loop(0, ch, unroll=8)
    def _(c):
        block_ref[0, c] = (
            frames_ref[0, c].astype(F32) + tmp[pl.ds(c, n, stride=ch), :]
        ).astype(BF16)

    many(kp, n - 1, 14).wait_recv()
    lags = jnp.sum(kp[...], axis=0)
    kernel_grad_ref[...] = jnp.concatenate([lags[:, :ch], lags[:, ch:]], axis=0)

    all_chunks(rred, n - 1, 10).wait_recv()
    for a in range(3):
        for b in range(3):
            rows = []
            for j in range(per):
                at = (a * 3 + b) * per + j
                rows.append(gathered[pl.ds(at, n, stride=pad), :])
            tap = jnp.concatenate(rows, axis=0)
            weight_grad_ref[a, b] = jnp.concatenate([tap[:, :ch], tap[:, ch:]], axis=0)

    all_of(rcot, 4).wait_send()
    all_of(ract, 5, 0, half).wait_send()
    all_of(ract, 11, half, half).wait_send()
    all_of(rback, 6).wait_send()
    all_of(ralong, 7, 0, half).wait_send()
    all_of(ralong, 12, half, half).wait_send()
    many(kz, zcount - 1, 13).wait_send()
    many(kp, n - 1, 14).wait_send()
    all_chunks(rred, n - 1, 8).wait_send()
    all_chunks(zpart, zcount - 1, 9).wait_send()
    all_chunks(rred, n - 1, 10).wait_send()


def store_kernel(*refs):
    count = len(refs) // 2
    sems = refs[-1]
    copies = [
        pltpu.make_async_copy(refs[k], refs[count + k], sems.at[k]) for k in range(count)
    ]
    for copy in copies:
        copy.start()
    for copy in copies:
        copy.wait()


def store(*arrays):
    count = len(arrays)
    return pl.pallas_call(
        store_kernel,
        name="store",
        out_shape=tuple(jax.ShapeDtypeStruct(x.shape, x.dtype) for x in arrays),
        in_specs=[pl.BlockSpec(memory_space=pl.ANY)] * count,
        out_specs=(pl.BlockSpec(memory_space=pl.ANY),) * count,
        scratch_shapes=[pltpu.SemaphoreType.DMA((count,))],
        compiler_params=pltpu.CompilerParams(vmem_limit_bytes=2**20),
    )(*arrays)


def local(frames, cotangent, spatial_weight, temporal_kernel):
    n = lax.axis_size("tm")
    nspan = lax.axis_size("span")
    _, ch, rows, width = frames.shape
    assert rows == n and ch == 64 and width == LANES and frames.shape[0] == 1
    gscale = float(n * rows * nspan * width) ** (-0.5)
    block = (n, ch, LANES)
    pad = (9 * (32 // n) + 7) // 8 * 8

    def vmem(shape, dtype):
        return pltpu.VMEM(shape, dtype)

    spec = pl.BlockSpec(memory_space=pltpu.VMEM)
    results = pl.pallas_call(
        functools.partial(kernel, n, nspan, gscale),
        name="space_time_block",
        out_shape=(
            jax.ShapeDtypeStruct(frames.shape, BF16),
            jax.ShapeDtypeStruct(frames.shape, BF16),
            jax.ShapeDtypeStruct((3, 3, ch, ch), F32),
            jax.ShapeDtypeStruct((n, ch), F32),
        ),
        in_specs=[pl.BlockSpec(memory_space=pltpu.HBM)] * 4,
        out_specs=(spec,) * 4,
        scratch_shapes=[
            vmem(frames.shape, BF16),
            vmem(frames.shape, BF16),
            vmem(spatial_weight.shape, BF16),
            vmem((n, ch), BF16),
            vmem((n * ch, LANES), F32),
            vmem((3 * ch, 3 * ch), BF16),
            vmem((3 * ch, 3 * ch), BF16),
            vmem((n + 2, ch, LANES), BF16),
            vmem((3 * ch, n * LANES), BF16),
            vmem(block, BF16),
            vmem(block, BF16),
            vmem(block, F32),
            vmem(block, F32),
            vmem(block, BF16),
            vmem(block, BF16),
            vmem(block, F32),
            vmem(block, F32),
            vmem(block, F32),
            vmem(block, BF16),
            vmem(block, BF16),
            vmem(block, BF16),
            vmem(block, BF16),
            vmem((n + 2, ch, LANES), BF16),
            vmem((3 * ch, n * LANES), BF16),
            vmem((n * ch, LANES), F32),
            vmem((ch, LANES), F32),
            vmem((nspan, n // 2, LANES), F32),
            vmem((n, n // 2, LANES), F32),
            vmem((n * pad, LANES), F32),
            vmem((n, pad, LANES), F32),
            vmem((pad, LANES), F32),
            vmem((nspan, pad, LANES), F32),
            vmem((pad, LANES), F32),
            vmem((n * pad, LANES), F32),
            pltpu.SemaphoreType.DMA((15,)),
            pltpu.SemaphoreType.DMA((15,)),
            pltpu.SemaphoreType.DMA((4,)),
        ],
        compiler_params=pltpu.CompilerParams(
            collective_id=0, has_side_effects=True, vmem_limit_bytes=52 * 2**20
        ),
    )(frames, cotangent, spatial_weight, temporal_kernel.T)
    block_output, input_grad, weight_grad, kernel_grad = store(*results)
    return block_output, input_grad, weight_grad, kernel_grad.T


def solution(mesh):
    placed = (P("tm", None, "span", None), P("tm", None, "span", None), P(), P())
    return jax.shard_map(
        local,
        mesh=mesh,
        in_specs=placed,
        out_specs=placed,
        check_vma=False,
    )
```

```python
import functools

import jax
import jax.numpy as jnp
from jax import lax
from jax.experimental import pallas as pl
from jax.experimental.pallas import tpu as pltpu
from jax.sharding import PartitionSpec as P

F32 = jnp.float32
BF16 = jnp.bfloat16
MESH = pl.DeviceIdType.MESH
LANES = 128
BLK = 8


def causal_sums(n, x_at, k_at, put):
    for tb in range(0, n, BLK):
        acc = [None] * BLK
        for rb in range(0, tb + BLK, BLK):
            xs = [x_at(rb + j) for j in range(BLK)]
            ks = {}
            for lag in range(max(0, tb - rb - BLK + 1), tb - rb + BLK):
                ks[lag] = k_at(lag)
            for i in range(BLK):
                for j in range(BLK):
                    lag = tb + i - rb - j
                    if lag >= 0:
                        term = ks[lag] * xs[j]
                        acc[i] = term if acc[i] is None else acc[i] + term
        for i in range(BLK):
            put(tb + i, acc[i])


def lag_sums(n, t_at, r_at, put):
    acc = {}
    for dist in range(0, n, BLK):
        for rb in range(0, n - dist, BLK):
            ts = [t_at(rb + dist + i) for i in range(BLK)]
            rs = [r_at(rb + j) for j in range(BLK)]
            for i in range(BLK):
                for j in range(BLK):
                    lag = dist + i - j
                    if lag >= 0:
                        term = ts[i] * rs[j]
                        acc[lag] = acc[lag] + term if lag in acc else term
        for lag in sorted(acc):
            if lag <= dist:
                put(lag, acc.pop(lag))
    for lag in sorted(acc):
        put(lag, acc.pop(lag))


def kernel(
    n,
    nspan,
    gscale,
    frames_hbm,
    cot_hbm,
    weight_hbm,
    temporal_hbm,
    block_ref,
    input_grad_ref,
    weight_grad_ref,
    kernel_grad_ref,
    frames_ref,
    cot_ref,
    weight_ref,
    temporal_ref,
    tmp,
    wf,
    wb,
    xp,
    x3,
    cot_t,
    act_t,
    gbuf,
    kb,
    rcot,
    ract,
    xf,
    yf,
    outf,
    back_t,
    along_t,
    rback,
    ralong,
    dp,
    db,
    igf,
    kgbuf,
    kz,
    kp,
    red,
    rred,
    part,
    zpart,
    full,
    gathered,
    send_sems,
    recv_sems,
    load_sems,
):
    me = lax.axis_index("tm")
    sp = lax.axis_index("span")
    xy, zh = me // 2, me % 2
    zl, core = sp // 2, sp % 2
    zcount = nspan
    zi = zh * (nspan // 2) + zl
    pi = xy * 2 + core
    ch = 64

    def tm_dev(t):
        return (t, sp)

    def plane_dev(p):
        return ((p // 2) * 2 + zh, zl * 2 + p % 2)

    def z_dev(z):
        return (xy * 2 + z // (nspan // 2), (z % (nspan // 2)) * 2 + core)

    loads = [
        pltpu.make_async_copy(src, dst, load_sems.at[k])
        for k, (src, dst) in enumerate(
            [
                (cot_hbm, cot_ref),
                (frames_hbm, frames_ref),
                (weight_hbm, weight_ref),
                (temporal_hbm, temporal_ref),
            ]
        )
    ]
    for load in loads:
        load.start()

    barrier = pltpu.get_barrier_semaphore()

    def greet(dev):
        pl.semaphore_signal(barrier, inc=1, device_id=dev, device_id_type=MESH)

    @pl.loop(1, n)
    def _(k):
        greet(tm_dev(lax.rem(me + k, n)))

    @pl.loop(0, n // 2)
    def _(k):
        greet(plane_dev(2 * lax.rem(xy + k, n // 2) + 1 - core))

    @pl.loop(1, zcount // 2)
    def _(k):
        greet(z_dev(lax.rem(zi + k, zcount)))
        greet(z_dev(lax.rem(zi + zcount - k, zcount)))

    greet((me, lax.rem(sp + 1, nspan)))
    greet((me, lax.rem(sp + nspan - 1, nspan)))

    lane = lax.broadcasted_iota(jnp.int32, (ch, LANES), 1)

    def right(v):
        return jnp.where(lane == 0, 0.0, pltpu.roll(v, 1, 1))

    def left(v):
        return jnp.where(lane == LANES - 1, 0.0, pltpu.roll(v, LANES - 1, 1))

    def rows_first(src, dst, offset):
        @pl.loop(0, ch, unroll=8)
        def _(c):
            tmp[pl.ds(c, n, stride=ch), :] = src[0, c].astype(F32)

        @pl.loop(0, n, unroll=4)
        def _(r):
            dst[r + offset] = tmp[pl.ds(pl.multiple_of(r * ch, ch), ch), :].astype(BF16)

    loads[0].wait()
    rows_first(cot_ref, cot_t, 0)
    loads[1].wait()
    rows_first(frames_ref, xp, 1)

    @pl.when(sp == 0)
    def _():
        xp[0] = jnp.zeros((ch, LANES), BF16)
        dp[0] = jnp.zeros((ch, LANES), BF16)

    @pl.when(sp == nspan - 1)
    def _():
        xp[n + 1] = jnp.zeros((ch, LANES), BF16)
        dp[n + 1] = jnp.zeros((ch, LANES), BF16)

    def row_cols(s):
        return pl.ds(pl.multiple_of(s * LANES, LANES), LANES)

    def load_taps(s):
        for a in range(3):
            x3[a * ch : (a + 1) * ch, row_cols(s)] = xp[s + a]

    def forward_rows(rows):
        taps = jnp.concatenate([x3[:, row_cols(s)] for s in rows], axis=1)
        out = jnp.dot(wf[...], taps, preferred_element_type=F32)
        for k, s in enumerate(rows):
            o = out[:, k * LANES : (k + 1) * LANES]
            hidden = o[ch : 2 * ch] + right(o[:ch]) + left(o[2 * ch :])
            sigma = jax.nn.sigmoid(hidden)
            act_t[s] = (hidden * sigma).astype(BF16)
            gbuf[s] = sigma * (1.0 + hidden * (1.0 - sigma))

    pl.semaphore_wait(barrier, n - 1 + n // 2 + 2 * (zcount // 2 - 1) + 2)

    def exchange(src, dst, idx, k, lo, size, near=None):
        peer = lax.rem(me + k, n)
        return pltpu.make_async_remote_copy(
            src_ref=src.at[peer, pl.ds(lo, size)],
            dst_ref=dst.at[me, pl.ds(lo, size)],
            send_sem=send_sems.at[idx],
            recv_sem=recv_sems.at[idx if near is None else near],
            device_id=tm_dev(peer),
            device_id_type=MESH,
        )

    def start_far(src, dst, idx, lo, size, first, last):
        @pl.loop(first, last)
        def _(k):
            exchange(src, dst, idx, 2 * k + 1, lo, size).start()

    def start_exchange(src, dst, idx, lo=0, size=64, held=0, near=None):
        start_far(src, dst, idx, lo, size, 0, n // 2 - held)

        @pl.loop(1, n // 2)
        def _(k):
            exchange(src, dst, idx, 2 * k, lo, size, near).start()

        dst[me, lo : lo + size] = src[me, lo : lo + size]

    def start_held(src, dst, idx, lo, size, held):
        start_far(src, dst, idx, lo, size, n // 2 - held, n // 2)

    def all_of(buf, idx, lo=0, size=64, count=n - 1):
        view = buf.at[pl.ds(0, count), pl.ds(lo, size)]
        return pltpu.make_async_remote_copy(
            src_ref=view,
            dst_ref=view,
            send_sem=send_sems.at[idx],
            recv_sem=recv_sems.at[idx],
            device_id=tm_dev(lax.rem(me + 1, n)),
            device_id_type=MESH,
        )

    def halo(buf, idx):
        up = pltpu.make_async_remote_copy(
            src_ref=buf.at[n],
            dst_ref=buf.at[0],
            send_sem=send_sems.at[idx],
            recv_sem=recv_sems.at[idx],
            device_id=(me, sp + 1),
            device_id_type=MESH,
        )
        down = pltpu.make_async_remote_copy(
            src_ref=buf.at[1],
            dst_ref=buf.at[n + 1],
            send_sem=send_sems.at[idx + 1],
            recv_sem=recv_sems.at[idx + 1],
            device_id=(me, sp - 1),
            device_id_type=MESH,
        )
        return up, down

    def start_halo(buf, idx):
        up, down = halo(buf, idx)

        @pl.when(sp < nspan - 1)
        def _():
            up.start()

        @pl.when(sp > 0)
        def _():
            down.start()

    def finish_halo(buf, idx):
        up, down = halo(buf, idx)

        @pl.when(sp > 0)
        def _():
            up.wait_recv()

        @pl.when(sp < nspan - 1)
        def _():
            down.wait_recv()

        @pl.when(sp < nspan - 1)
        def _():
            up.wait_send()

        @pl.when(sp > 0)
        def _():
            down.wait_send()

    start_halo(xp, 0)
    half = ch // 2
    start_exchange(cot_t, rcot, 4, 0, half)
    start_exchange(cot_t, rcot, 15, half, half)

    loads[2].wait()
    loads[3].wait()
    wide = []
    for b in range(3):
        wide.append(jnp.concatenate([weight_ref[a, b].astype(F32) for a in range(3)], axis=1))
    wf[...] = jnp.concatenate(wide, axis=0).astype(BF16)
    wide = []
    for j in range(3):
        wide.append(jnp.concatenate([weight_ref[2 - j, b].astype(F32) for b in range(3)], axis=1))
    wb[...] = jnp.concatenate(wide, axis=0).T.astype(BF16)

    @pl.loop(1, n - 1, unroll=2)
    def _(s):
        load_taps(s)


    @pl.loop(0, (n - 2) // 2, unroll=3)
    def _(p):
        forward_rows([1 + 2 * p, 2 + 2 * p])

    finish_halo(xp, 0)
    load_taps(0)
    load_taps(n - 1)
    forward_rows([0, n - 1])

    columns = temporal_ref[...].astype(F32).T
    for lag in range(n):
        kb[lag] = jnp.broadcast_to(columns[:, lag : lag + 1], (ch, LANES))

    def chan(c):
        return pl.ds(pl.multiple_of(c * 8, 8), 8)

    def back_half(h, in_idx, out_idx):
        lo = h * half
        all_of(rcot, in_idx, lo, half).wait_recv()

        @pl.loop(0, n, unroll=4)
        def _(t):
            yf[t, lo : lo + half] = rcot[t, lo : lo + half].astype(F32)

        @pl.loop(h * (half // 8), (h + 1) * (half // 8))
        def _(c):
            def put(t, v):
                outf[n - 1 - t, chan(c), :] = v

            causal_sums(
                n, lambda t: yf[n - 1 - t, chan(c), :], lambda lag: kb[lag, chan(c), :], put
            )

        @pl.loop(0, n, unroll=4)
        def _(t):
            back_t[t, lo : lo + half] = outf[t, lo : lo + half].astype(BF16)

        start_exchange(back_t, rback, out_idx, lo, half, near=17 + h)

    back_half(0, 4, 6)
    back_half(1, 15, 16)
    start_exchange(act_t, ract, 5, 0, half)
    start_exchange(act_t, ract, 11, half, half, held=n * 0 // 32)

    lane8 = lax.broadcasted_iota(jnp.int32, (8, LANES), 1)

    def take_act(h, in_idx):
        lo = h * half
        all_of(ract, in_idx, lo, half).wait_recv()

        @pl.loop(0, n, unroll=4)
        def _(t):
            xf[t, lo : lo + half] = ract[t, lo : lo + half].astype(F32)

    def along_half(h, out_idx, held=0):
        lo = h * half

        @pl.loop(h * (half // 8), (h + 1) * (half // 8))
        def _(c):
            def put(t, v):
                outf[t, chan(c), :] = v

            causal_sums(n, lambda t: xf[t, chan(c), :], lambda lag: kb[lag, chan(c), :], put)

        @pl.loop(0, n, unroll=4)
        def _(t):
            along_t[t, lo : lo + half] = outf[t, lo : lo + half].astype(BF16)

        start_exchange(along_t, ralong, out_idx, lo, half, held=held)

    def lag_half(h):
        @pl.loop(h * (half // 8), (h + 1) * (half // 8))
        def _(c):
            total = [jnp.zeros((8, LANES), F32)]

            def put(lag, v):
                row = jnp.sum(v, axis=1, keepdims=True)
                total[0] = jnp.where(lane8 == lag, row, total[0])

            lag_sums(n, lambda t: yf[t, chan(c), :], lambda r: xf[r, chan(c), :], put)
            kgbuf[chan(c), :] = total[0]

    def gate_row(s):
        v = rback[s].astype(F32) * gbuf[s]
        dp[s + 1] = v.astype(BF16)
        db[:ch, row_cols(s)] = left(v).astype(BF16)
        db[ch : 2 * ch, row_cols(s)] = v.astype(BF16)
        db[2 * ch :, row_cols(s)] = right(v).astype(BF16)

    all_of(rback, 17, 0, half, n // 2 - 1).wait_recv()
    all_of(rback, 18, half, half, n // 2 - 1).wait_recv()

    @pl.loop(0, n // 2, unroll=4)
    def _(k):
        gate_row(2 * k + zh)

    all_of(rback, 6, 0, half, n // 2).wait_recv()
    all_of(rback, 16, half, half, n // 2).wait_recv()

    @pl.loop(0, n // 2, unroll=4)
    def _(k):
        gate_row(2 * k + 1 - zh)

    start_halo(dp, 2)

    grads = lax.dot_general(
        db[...], x3[...], (((1,), (1,)), ((), ())), preferred_element_type=F32
    )
    per = 32 // n
    used = 9 * per
    pad = (used + 7) // 8 * 8
    for a in range(3):
        for b in range(3):
            tap = grads[b * ch : (b + 1) * ch, a * ch : (a + 1) * ch]
            tap = jnp.concatenate([tap[: ch // 2], tap[ch // 2 :]], axis=1)
            for j in range(per):
                at = (a * 3 + b) * per + j
                red[pl.ds(at, n, stride=pad), :] = tap[j * n : (j + 1) * n]

    def chunk(buf, k):
        return buf.at[pl.ds(pl.multiple_of(k * pad, pad), used)]

    def plane_copy(src, dst, idx, peer):
        return pltpu.make_async_remote_copy(
            src_ref=src,
            dst_ref=dst,
            send_sem=send_sems.at[idx],
            recv_sem=recv_sems.at[idx],
            device_id=plane_dev(peer),
            device_id_type=MESH,
        )

    @pl.loop(1, n)
    def _(k):
        peer = lax.rem(pi + k, n)
        plane_copy(chunk(red, peer), rred.at[pi, pl.ds(0, used)], 8, peer).start()

    start_held(act_t, ract, 11, half, half, n * 0 // 32)
    rred[pi, 0:used, :] = red[pl.ds(pl.multiple_of(pi * pad, pad), used), :]

    def backward_rows(rows):
        taps = jnp.concatenate(
            [jnp.concatenate([dp[s + j] for j in range(3)], axis=0) for s in rows], axis=1
        )
        out = jnp.dot(wb[...], taps, preferred_element_type=F32)
        for k, s in enumerate(rows):
            o = out[:, k * LANES : (k + 1) * LANES]
            igf[pl.ds(pl.multiple_of(s * ch, ch), ch), :] = (
                o[ch : 2 * ch] + left(o[:ch]) + right(o[2 * ch :])
            )

    take_act(0, 5)
    along_half(0, 7)

    @pl.loop(0, (n - 2) // 2, unroll=3)
    def _(p):
        backward_rows([1 + 2 * p, 2 + 2 * p])

    lag_half(0)

    def many(buf, count, idx):
        view = buf.at[pl.ds(0, count)]
        return plane_copy(view, view, idx, lax.rem(pi + 1, n))

    def all_chunks(buf, count, idx):
        view = buf.at[pl.ds(0, count), pl.ds(0, used)]
        return plane_copy(view, view, idx, lax.rem(pi + 1, n))

    all_chunks(rred, n - 1, 8).wait_recv()
    part[0:used, :] = jnp.sum(rred[:, 0:used, :], axis=0)

    def z_copy(src, dst, idx, k):
        return pltpu.make_async_remote_copy(
            src_ref=src,
            dst_ref=dst,
            send_sem=send_sems.at[idx],
            recv_sem=recv_sems.at[idx],
            device_id=z_dev(lax.rem(zi + k, zcount)),
            device_id_type=MESH,
        )

    @pl.loop(1, zcount)
    def _(k):
        z_copy(part.at[pl.ds(0, used)], zpart.at[zi, pl.ds(0, used)], 9, k).start()

    zpart[zi, 0:used, :] = part[0:used, :]

    take_act(1, 11)
    lag_half(1)
    lags = kgbuf[...].T[:n]
    kz[zi] = jnp.concatenate([lags[: n // 2], lags[n // 2 :]], axis=1)

    @pl.loop(1, zcount)
    def _(k):
        z_copy(kz.at[zi], kz.at[zi], 13, k).start()

    along_half(1, 12, held=n * 8 // 32)

    finish_halo(dp, 2)
    backward_rows([0, n - 1])

    all_chunks(zpart, zcount - 1, 9).wait_recv()
    full[0:used, :] = jnp.sum(zpart[:, 0:used, :], axis=0) * gscale

    @pl.loop(1, n)
    def _(k):
        peer = lax.rem(pi + k, n)
        plane_copy(full.at[pl.ds(0, used)], chunk(gathered, pi), 10, peer).start()

    gathered[pl.ds(pl.multiple_of(pi * pad, pad), used), :] = full[0:used, :]

    many(kz, zcount - 1, 13).wait_recv()
    kp[pi] = jnp.sum(kz[...], axis=0) * gscale

    @pl.loop(1, n)
    def _(k):
        plane_copy(kp.at[pi], kp.at[pi], 14, lax.rem(pi + k, n)).start()

    start_held(along_t, ralong, 12, half, half, n * 8 // 32)

    @pl.loop(0, ch, unroll=8)
    def _(c):
        input_grad_ref[0, c] = (
            cot_ref[0, c].astype(F32) + igf[pl.ds(c, n, stride=ch), :]
        ).astype(BF16)

    def output_half(h, idx):
        lo = h * half
        all_of(ralong, idx, lo, half).wait_recv()

        @pl.loop(0, n, unroll=4)
        def _(r):
            tmp[pl.ds(pl.multiple_of(r * ch + lo, half), half), :] = ralong[
                r, lo : lo + half
            ].astype(F32)

        @pl.loop(lo, lo + half, unroll=8)
        def _(c):
            block_ref[0, c] = (
                frames_ref[0, c].astype(F32) + tmp[pl.ds(c, n, stride=ch), :]
            ).astype(BF16)

    output_half(0, 7)

    many(kp, n - 1, 14).wait_recv()
    lags = jnp.sum(kp[...], axis=0)
    kernel_grad_ref[...] = jnp.concatenate([lags[:, :ch], lags[:, ch:]], axis=0)

    all_chunks(rred, n - 1, 10).wait_recv()
    for a in range(3):
        for b in range(3):
            rows = []
            for j in range(per):
                at = (a * 3 + b) * per + j
                rows.append(gathered[pl.ds(at, n, stride=pad), :])
            tap = jnp.concatenate(rows, axis=0)
            weight_grad_ref[a, b] = jnp.concatenate([tap[:, :ch], tap[:, ch:]], axis=0)

    output_half(1, 12)

    for buf, low, high in ((rcot, 4, 15), (rback, 6, 16), (ract, 5, 11), (ralong, 7, 12)):
        all_of(buf, low, 0, half).wait_send()
        all_of(buf, high, half, half).wait_send()
    many(kz, zcount - 1, 13).wait_send()
    many(kp, n - 1, 14).wait_send()
    all_chunks(rred, n - 1, 8).wait_send()
    all_chunks(zpart, zcount - 1, 9).wait_send()
    all_chunks(rred, n - 1, 10).wait_send()


def store_kernel(*refs):
    count = len(refs) // 2
    sems = refs[-1]
    copies = [
        pltpu.make_async_copy(refs[k], refs[count + k], sems.at[k]) for k in range(count)
    ]
    for copy in copies:
        copy.start()
    for copy in copies:
        copy.wait()


def store(*arrays):
    count = len(arrays)
    return pl.pallas_call(
        store_kernel,
        name="store",
        out_shape=tuple(jax.ShapeDtypeStruct(x.shape, x.dtype) for x in arrays),
        in_specs=[pl.BlockSpec(memory_space=pl.ANY)] * count,
        out_specs=(pl.BlockSpec(memory_space=pl.ANY),) * count,
        scratch_shapes=[pltpu.SemaphoreType.DMA((count,))],
        compiler_params=pltpu.CompilerParams(vmem_limit_bytes=2**20),
    )(*arrays)


def local(frames, cotangent, spatial_weight, temporal_kernel):
    n = lax.axis_size("tm")
    nspan = lax.axis_size("span")
    _, ch, rows, width = frames.shape
    assert rows == n and ch == 64 and width == LANES and frames.shape[0] == 1
    gscale = float(n * rows * nspan * width) ** (-0.5)
    block = (n, ch, LANES)
    pad = (9 * (32 // n) + 7) // 8 * 8

    def vmem(shape, dtype):
        return pltpu.VMEM(shape, dtype)

    spec = pl.BlockSpec(memory_space=pltpu.VMEM)
    results = pl.pallas_call(
        functools.partial(kernel, n, nspan, gscale),
        name="space_time_block",
        out_shape=(
            jax.ShapeDtypeStruct(frames.shape, BF16),
            jax.ShapeDtypeStruct(frames.shape, BF16),
            jax.ShapeDtypeStruct((3, 3, ch, ch), F32),
            jax.ShapeDtypeStruct((n, ch), F32),
        ),
        in_specs=[pl.BlockSpec(memory_space=pltpu.HBM)] * 4,
        out_specs=(spec,) * 4,
        scratch_shapes=[
            vmem(frames.shape, BF16),
            vmem(frames.shape, BF16),
            vmem(spatial_weight.shape, BF16),
            vmem((n, ch), BF16),
            vmem((n * ch, LANES), F32),
            vmem((3 * ch, 3 * ch), BF16),
            vmem((3 * ch, 3 * ch), BF16),
            vmem((n + 2, ch, LANES), BF16),
            vmem((3 * ch, n * LANES), BF16),
            vmem(block, BF16),
            vmem(block, BF16),
            vmem(block, F32),
            vmem(block, F32),
            vmem(block, BF16),
            vmem(block, BF16),
            vmem(block, F32),
            vmem(block, F32),
            vmem(block, F32),
            vmem(block, BF16),
            vmem(block, BF16),
            vmem(block, BF16),
            vmem(block, BF16),
            vmem((n + 2, ch, LANES), BF16),
            vmem((3 * ch, n * LANES), BF16),
            vmem((n * ch, LANES), F32),
            vmem((ch, LANES), F32),
            vmem((nspan, n // 2, LANES), F32),
            vmem((n, n // 2, LANES), F32),
            vmem((n * pad, LANES), F32),
            vmem((n, pad, LANES), F32),
            vmem((pad, LANES), F32),
            vmem((nspan, pad, LANES), F32),
            vmem((pad, LANES), F32),
            vmem((n * pad, LANES), F32),
            pltpu.SemaphoreType.DMA((19,)),
            pltpu.SemaphoreType.DMA((19,)),
            pltpu.SemaphoreType.DMA((4,)),
        ],
        compiler_params=pltpu.CompilerParams(
            collective_id=0, has_side_effects=True, vmem_limit_bytes=50 * 2**20
        ),
    )(
        *[
            pltpu.with_memory_space_constraint(x, pltpu.HBM)
            for x in (frames, cotangent, spatial_weight, temporal_kernel.T)
        ]
    )
    block_output, input_grad, weight_grad, kernel_grad = store(*results)
    return block_output, input_grad, weight_grad, kernel_grad.T


def solution(mesh):
    placed = (P("tm", None, "span", None), P("tm", None, "span", None), P(), P())
    return jax.shard_map(
        local,
        mesh=mesh,
        in_specs=placed,
        out_specs=placed,
        check_vma=False,
    )
```

```python
import functools

import jax
import jax.numpy as jnp
from jax import lax
from jax.experimental import pallas as pl
from jax.experimental.pallas import tpu as pltpu
from jax.sharding import PartitionSpec as P

F32 = jnp.float32
BF16 = jnp.bfloat16
MESH = pl.DeviceIdType.MESH
LANES = 128
BLK = 8


def causal_sums(n, x_at, k_at, put):
    for tb in range(0, n, BLK):
        acc = [None] * BLK
        for rb in range(0, tb + BLK, BLK):
            xs = [x_at(rb + j) for j in range(BLK)]
            ks = {}
            for lag in range(max(0, tb - rb - BLK + 1), tb - rb + BLK):
                ks[lag] = k_at(lag)
            for i in range(BLK):
                for j in range(BLK):
                    lag = tb + i - rb - j
                    if lag >= 0:
                        term = ks[lag] * xs[j]
                        acc[i] = term if acc[i] is None else acc[i] + term
        for i in range(BLK):
            put(tb + i, acc[i])


def lag_sums(n, t_at, r_at, put):
    acc = {}
    for dist in range(0, n, BLK):
        for rb in range(0, n - dist, BLK):
            ts = [t_at(rb + dist + i) for i in range(BLK)]
            rs = [r_at(rb + j) for j in range(BLK)]
            for i in range(BLK):
                for j in range(BLK):
                    lag = dist + i - j
                    if lag >= 0:
                        term = ts[i] * rs[j]
                        acc[lag] = acc[lag] + term if lag in acc else term
        for lag in sorted(acc):
            if lag <= dist:
                put(lag, acc.pop(lag))
    for lag in sorted(acc):
        put(lag, acc.pop(lag))


def kernel(
    n,
    nspan,
    gscale,
    frames_hbm,
    cot_hbm,
    weight_hbm,
    temporal_hbm,
    block_ref,
    input_grad_ref,
    weight_grad_ref,
    kernel_grad_ref,
    frames_ref,
    cot_ref,
    weight_ref,
    temporal_ref,
    tmp,
    wf,
    wb,
    xp,
    x3,
    cot_t,
    act_t,
    gbuf,
    kb,
    rcot,
    ract,
    xf,
    yf,
    outf,
    back_t,
    along_t,
    rback,
    ralong,
    dp,
    db,
    igf,
    kgbuf,
    kz,
    kp,
    red,
    rred,
    part,
    zpart,
    full,
    gathered,
    send_sems,
    recv_sems,
    load_sems,
):
    me = lax.axis_index("tm")
    sp = lax.axis_index("span")
    xy, zh = me // 2, me % 2
    zl, core = sp // 2, sp % 2
    zcount = nspan
    zi = zh * (nspan // 2) + zl
    pi = xy * 2 + core
    ch = 64

    def tm_dev(t):
        return (t, sp)

    def plane_dev(p):
        return ((p // 2) * 2 + zh, zl * 2 + p % 2)

    def z_dev(z):
        return (xy * 2 + z // (nspan // 2), (z % (nspan // 2)) * 2 + core)

    loads = [
        pltpu.make_async_copy(src, dst, load_sems.at[k])
        for k, (src, dst) in enumerate(
            [
                (cot_hbm, cot_ref),
                (frames_hbm, frames_ref),
                (weight_hbm, weight_ref),
                (temporal_hbm, temporal_ref),
            ]
        )
    ]
    for load in loads:
        load.start()

    barrier = pltpu.get_barrier_semaphore()

    def greet(dev):
        pl.semaphore_signal(barrier, inc=1, device_id=dev, device_id_type=MESH)

    @pl.loop(1, n)
    def _(k):
        greet(tm_dev(lax.rem(me + k, n)))

    @pl.loop(0, n // 2)
    def _(k):
        greet(plane_dev(2 * lax.rem(xy + k, n // 2) + 1 - core))

    @pl.loop(1, zcount // 2)
    def _(k):
        greet(z_dev(lax.rem(zi + k, zcount)))
        greet(z_dev(lax.rem(zi + zcount - k, zcount)))

    greet((me, lax.rem(sp + 1, nspan)))
    greet((me, lax.rem(sp + nspan - 1, nspan)))

    lane = lax.broadcasted_iota(jnp.int32, (ch, LANES), 1)

    def right(v):
        return jnp.where(lane == 0, 0.0, pltpu.roll(v, 1, 1))

    def left(v):
        return jnp.where(lane == LANES - 1, 0.0, pltpu.roll(v, LANES - 1, 1))

    def rows_first(src, dst, offset):
        @pl.loop(0, ch, unroll=8)
        def _(c):
            tmp[pl.ds(c, n, stride=ch), :] = src[0, c].astype(F32)

        @pl.loop(0, n, unroll=4)
        def _(r):
            dst[r + offset] = tmp[pl.ds(pl.multiple_of(r * ch, ch), ch), :].astype(BF16)

    loads[0].wait()
    rows_first(cot_ref, cot_t, 0)
    loads[1].wait()
    rows_first(frames_ref, xp, 1)

    @pl.when(sp == 0)
    def _():
        xp[0] = jnp.zeros((ch, LANES), BF16)
        dp[0] = jnp.zeros((ch, LANES), BF16)

    @pl.when(sp == nspan - 1)
    def _():
        xp[n + 1] = jnp.zeros((ch, LANES), BF16)
        dp[n + 1] = jnp.zeros((ch, LANES), BF16)

    def row_cols(s):
        return pl.ds(pl.multiple_of(s * LANES, LANES), LANES)

    def load_taps(s):
        for a in range(3):
            x3[a * ch : (a + 1) * ch, row_cols(s)] = xp[s + a]

    def forward_rows(rows):
        taps = jnp.concatenate([x3[:, row_cols(s)] for s in rows], axis=1)
        out = jnp.dot(wf[...], taps, preferred_element_type=F32)
        for k, s in enumerate(rows):
            o = out[:, k * LANES : (k + 1) * LANES]
            hidden = o[ch : 2 * ch] + right(o[:ch]) + left(o[2 * ch :])
            sigma = jax.nn.sigmoid(hidden)
            act_t[s] = (hidden * sigma).astype(BF16)
            gbuf[s] = sigma * (1.0 + hidden * (1.0 - sigma))

    pl.semaphore_wait(barrier, n - 1 + n // 2 + 2 * (zcount // 2 - 1) + 2)

    def exchange(src, dst, idx, k, lo, size):
        peer = lax.rem(me + k, n)
        return pltpu.make_async_remote_copy(
            src_ref=src.at[peer, pl.ds(lo, size)],
            dst_ref=dst.at[me, pl.ds(lo, size)],
            send_sem=send_sems.at[idx],
            recv_sem=recv_sems.at[idx],
            device_id=tm_dev(peer),
            device_id_type=MESH,
        )

    def start_far(src, dst, idx, lo, size, first, last):
        @pl.loop(first, last)
        def _(k):
            exchange(src, dst, idx, 2 * k + 1, lo, size).start()

    def start_exchange(src, dst, idx, lo=0, size=64, held=0):
        start_far(src, dst, idx, lo, size, 0, n // 2 - held)

        @pl.loop(1, n // 2)
        def _(k):
            exchange(src, dst, idx, 2 * k, lo, size).start()

        dst[me, lo : lo + size] = src[me, lo : lo + size]

    def start_held(src, dst, idx, lo, size, held):
        start_far(src, dst, idx, lo, size, n // 2 - held, n // 2)

    def all_of(buf, idx, lo=0, size=64):
        view = buf.at[pl.ds(0, n - 1), pl.ds(lo, size)]
        return pltpu.make_async_remote_copy(
            src_ref=view,
            dst_ref=view,
            send_sem=send_sems.at[idx],
            recv_sem=recv_sems.at[idx],
            device_id=tm_dev(lax.rem(me + 1, n)),
            device_id_type=MESH,
        )

    def halo(buf, idx):
        up = pltpu.make_async_remote_copy(
            src_ref=buf.at[n],
            dst_ref=buf.at[0],
            send_sem=send_sems.at[idx],
            recv_sem=recv_sems.at[idx],
            device_id=(me, sp + 1),
            device_id_type=MESH,
        )
        down = pltpu.make_async_remote_copy(
            src_ref=buf.at[1],
            dst_ref=buf.at[n + 1],
            send_sem=send_sems.at[idx + 1],
            recv_sem=recv_sems.at[idx + 1],
            device_id=(me, sp - 1),
            device_id_type=MESH,
        )
        return up, down

    def start_halo(buf, idx):
        up, down = halo(buf, idx)

        @pl.when(sp < nspan - 1)
        def _():
            up.start()

        @pl.when(sp > 0)
        def _():
            down.start()

    def finish_halo(buf, idx):
        up, down = halo(buf, idx)

        @pl.when(sp > 0)
        def _():
            up.wait_recv()

        @pl.when(sp < nspan - 1)
        def _():
            down.wait_recv()

        @pl.when(sp < nspan - 1)
        def _():
            up.wait_send()

        @pl.when(sp > 0)
        def _():
            down.wait_send()

    start_halo(xp, 0)
    half = ch // 4
    cot_sems, back_sems, act_sems, along_sems = (4, 15, 17, 18), (6, 16, 19, 20), (5, 11, 21, 22), (7, 12, 23, 24)
    for h in range(4):
        start_exchange(cot_t, rcot, cot_sems[h], h * half, half)

    loads[2].wait()
    loads[3].wait()
    wide = []
    for b in range(3):
        wide.append(jnp.concatenate([weight_ref[a, b].astype(F32) for a in range(3)], axis=1))
    wf[...] = jnp.concatenate(wide, axis=0).astype(BF16)
    wide = []
    for j in range(3):
        wide.append(jnp.concatenate([weight_ref[2 - j, b].astype(F32) for b in range(3)], axis=1))
    wb[...] = jnp.concatenate(wide, axis=0).T.astype(BF16)

    @pl.loop(1, n - 1, unroll=2)
    def _(s):
        load_taps(s)


    @pl.loop(0, (n - 2) // 2, unroll=3)
    def _(p):
        forward_rows([1 + 2 * p, 2 + 2 * p])

    finish_halo(xp, 0)
    load_taps(0)
    load_taps(n - 1)
    forward_rows([0, n - 1])

    columns = temporal_ref[...].astype(F32).T
    for lag in range(n):
        kb[lag] = jnp.broadcast_to(columns[:, lag : lag + 1], (ch, LANES))

    def chan(c):
        return pl.ds(pl.multiple_of(c * 8, 8), 8)

    def back_half(h, in_idx, out_idx):
        lo = h * half
        all_of(rcot, in_idx, lo, half).wait_recv()

        @pl.loop(0, n, unroll=4)
        def _(t):
            yf[t, lo : lo + half] = rcot[t, lo : lo + half].astype(F32)

        @pl.loop(h * (half // 8), (h + 1) * (half // 8))
        def _(c):
            def put(t, v):
                outf[n - 1 - t, chan(c), :] = v

            causal_sums(
                n, lambda t: yf[n - 1 - t, chan(c), :], lambda lag: kb[lag, chan(c), :], put
            )

        @pl.loop(0, n, unroll=4)
        def _(t):
            back_t[t, lo : lo + half] = outf[t, lo : lo + half].astype(BF16)

        start_exchange(back_t, rback, out_idx, lo, half)

    for h in range(4):
        back_half(h, cot_sems[h], back_sems[h])
    for h in range(4):
        start_exchange(act_t, ract, act_sems[h], h * half, half)

    lane8 = lax.broadcasted_iota(jnp.int32, (8, LANES), 1)

    def take_act(h, in_idx):
        lo = h * half
        all_of(ract, in_idx, lo, half).wait_recv()

        @pl.loop(0, n, unroll=4)
        def _(t):
            xf[t, lo : lo + half] = ract[t, lo : lo + half].astype(F32)

    def along_half(h, out_idx, held=0):
        lo = h * half

        @pl.loop(h * (half // 8), (h + 1) * (half // 8))
        def _(c):
            def put(t, v):
                outf[t, chan(c), :] = v

            causal_sums(n, lambda t: xf[t, chan(c), :], lambda lag: kb[lag, chan(c), :], put)

        @pl.loop(0, n, unroll=4)
        def _(t):
            along_t[t, lo : lo + half] = outf[t, lo : lo + half].astype(BF16)

        start_exchange(along_t, ralong, out_idx, lo, half, held=held)

    def lag_half(h):
        @pl.loop(h * (half // 8), (h + 1) * (half // 8))
        def _(c):
            total = [jnp.zeros((8, LANES), F32)]

            def put(lag, v):
                row = jnp.sum(v, axis=1, keepdims=True)
                total[0] = jnp.where(lane8 == lag, row, total[0])

            lag_sums(n, lambda t: yf[t, chan(c), :], lambda r: xf[r, chan(c), :], put)
            kgbuf[chan(c), :] = total[0]

    for h in range(4):
        all_of(rback, back_sems[h], h * half, half).wait_recv()

    def gate_row(s):
        v = rback[s].astype(F32) * gbuf[s]
        dp[s + 1] = v.astype(BF16)
        db[:ch, row_cols(s)] = left(v).astype(BF16)
        db[ch : 2 * ch, row_cols(s)] = v.astype(BF16)
        db[2 * ch :, row_cols(s)] = right(v).astype(BF16)

    gate_row(0)
    gate_row(n - 1)
    start_halo(dp, 2)

    @pl.loop(1, n - 1, unroll=5 if (n - 2) % 5 == 0 else 2)
    def _(s):
        gate_row(s)

    grads = lax.dot_general(
        db[...], x3[...], (((1,), (1,)), ((), ())), preferred_element_type=F32
    )
    per = 32 // n
    used = 9 * per
    pad = (used + 7) // 8 * 8
    for a in range(3):
        for b in range(3):
            tap = grads[b * ch : (b + 1) * ch, a * ch : (a + 1) * ch]
            tap = jnp.concatenate([tap[: ch // 2], tap[ch // 2 :]], axis=1)
            for j in range(per):
                at = (a * 3 + b) * per + j
                red[pl.ds(at, n, stride=pad), :] = tap[j * n : (j + 1) * n]

    def chunk(buf, k):
        return buf.at[pl.ds(pl.multiple_of(k * pad, pad), used)]

    def plane_copy(src, dst, idx, peer):
        return pltpu.make_async_remote_copy(
            src_ref=src,
            dst_ref=dst,
            send_sem=send_sems.at[idx],
            recv_sem=recv_sems.at[idx],
            device_id=plane_dev(peer),
            device_id_type=MESH,
        )

    @pl.loop(1, n)
    def _(k):
        peer = lax.rem(pi + k, n)
        plane_copy(chunk(red, peer), rred.at[pi, pl.ds(0, used)], 8, peer).start()

    rred[pi, 0:used, :] = red[pl.ds(pl.multiple_of(pi * pad, pad), used), :]

    def backward_rows(rows):
        taps = jnp.concatenate(
            [jnp.concatenate([dp[s + j] for j in range(3)], axis=0) for s in rows], axis=1
        )
        out = jnp.dot(wb[...], taps, preferred_element_type=F32)
        for k, s in enumerate(rows):
            o = out[:, k * LANES : (k + 1) * LANES]
            igf[pl.ds(pl.multiple_of(s * ch, ch), ch), :] = (
                o[ch : 2 * ch] + left(o[:ch]) + right(o[2 * ch :])
            )

    for h in range(2):
        take_act(h, act_sems[h])
        along_half(h, along_sems[h])

    @pl.loop(0, (n - 2) // 2, unroll=3)
    def _(p):
        backward_rows([1 + 2 * p, 2 + 2 * p])

    lag_half(0)
    lag_half(1)
    take_act(2, act_sems[2])
    along_half(2, along_sems[2])
    lag_half(2)

    def many(buf, count, idx):
        view = buf.at[pl.ds(0, count)]
        return plane_copy(view, view, idx, lax.rem(pi + 1, n))

    def all_chunks(buf, count, idx):
        view = buf.at[pl.ds(0, count), pl.ds(0, used)]
        return plane_copy(view, view, idx, lax.rem(pi + 1, n))

    all_chunks(rred, n - 1, 8).wait_recv()
    part[0:used, :] = jnp.sum(rred[:, 0:used, :], axis=0)

    def z_copy(src, dst, idx, k):
        return pltpu.make_async_remote_copy(
            src_ref=src,
            dst_ref=dst,
            send_sem=send_sems.at[idx],
            recv_sem=recv_sems.at[idx],
            device_id=z_dev(lax.rem(zi + k, zcount)),
            device_id_type=MESH,
        )

    @pl.loop(1, zcount)
    def _(k):
        z_copy(part.at[pl.ds(0, used)], zpart.at[zi, pl.ds(0, used)], 9, k).start()

    zpart[zi, 0:used, :] = part[0:used, :]

    take_act(3, act_sems[3])
    lag_half(3)
    lags = kgbuf[...].T[:n]
    kz[zi] = jnp.concatenate([lags[: n // 2], lags[n // 2 :]], axis=1)

    @pl.loop(1, zcount)
    def _(k):
        z_copy(kz.at[zi], kz.at[zi], 13, k).start()

    along_half(3, along_sems[3], held=n * 8 // 32)

    finish_halo(dp, 2)
    backward_rows([0, n - 1])

    all_chunks(zpart, zcount - 1, 9).wait_recv()
    full[0:used, :] = jnp.sum(zpart[:, 0:used, :], axis=0) * gscale

    @pl.loop(1, n)
    def _(k):
        peer = lax.rem(pi + k, n)
        plane_copy(full.at[pl.ds(0, used)], chunk(gathered, pi), 10, peer).start()

    gathered[pl.ds(pl.multiple_of(pi * pad, pad), used), :] = full[0:used, :]

    many(kz, zcount - 1, 13).wait_recv()
    kp[pi] = jnp.sum(kz[...], axis=0) * gscale

    @pl.loop(1, n)
    def _(k):
        plane_copy(kp.at[pi], kp.at[pi], 14, lax.rem(pi + k, n)).start()

    start_held(along_t, ralong, along_sems[3], 3 * half, half, n * 8 // 32)

    @pl.loop(0, ch, unroll=8)
    def _(c):
        input_grad_ref[0, c] = (
            cot_ref[0, c].astype(F32) + igf[pl.ds(c, n, stride=ch), :]
        ).astype(BF16)

    def output_half(h, idx):
        lo = h * half
        all_of(ralong, idx, lo, half).wait_recv()

        @pl.loop(0, n, unroll=4)
        def _(r):
            tmp[pl.ds(pl.multiple_of(r * ch + lo, half), half), :] = ralong[
                r, lo : lo + half
            ].astype(F32)

        @pl.loop(lo, lo + half, unroll=8)
        def _(c):
            block_ref[0, c] = (
                frames_ref[0, c].astype(F32) + tmp[pl.ds(c, n, stride=ch), :]
            ).astype(BF16)

    for h in range(3):
        output_half(h, along_sems[h])

    many(kp, n - 1, 14).wait_recv()
    lags = jnp.sum(kp[...], axis=0)
    kernel_grad_ref[...] = jnp.concatenate([lags[:, :ch], lags[:, ch:]], axis=0)

    all_chunks(rred, n - 1, 10).wait_recv()
    for a in range(3):
        for b in range(3):
            rows = []
            for j in range(per):
                at = (a * 3 + b) * per + j
                rows.append(gathered[pl.ds(at, n, stride=pad), :])
            tap = jnp.concatenate(rows, axis=0)
            weight_grad_ref[a, b] = jnp.concatenate([tap[:, :ch], tap[:, ch:]], axis=0)

    output_half(3, along_sems[3])

    for buf, sems in ((rcot, cot_sems), (rback, back_sems), (ract, act_sems), (ralong, along_sems)):
        for h in range(4):
            all_of(buf, sems[h], h * half, half).wait_send()
    many(kz, zcount - 1, 13).wait_send()
    many(kp, n - 1, 14).wait_send()
    all_chunks(rred, n - 1, 8).wait_send()
    all_chunks(zpart, zcount - 1, 9).wait_send()
    all_chunks(rred, n - 1, 10).wait_send()


def store_kernel(*refs):
    count = len(refs) // 2
    sems = refs[-1]
    copies = [
        pltpu.make_async_copy(refs[k], refs[count + k], sems.at[k]) for k in range(count)
    ]
    for copy in copies:
        copy.start()
    for copy in copies:
        copy.wait()


def store(*arrays):
    count = len(arrays)
    return pl.pallas_call(
        store_kernel,
        name="store",
        out_shape=tuple(jax.ShapeDtypeStruct(x.shape, x.dtype) for x in arrays),
        in_specs=[pl.BlockSpec(memory_space=pl.ANY)] * count,
        out_specs=(pl.BlockSpec(memory_space=pl.ANY),) * count,
        scratch_shapes=[pltpu.SemaphoreType.DMA((count,))],
        compiler_params=pltpu.CompilerParams(vmem_limit_bytes=2**20),
    )(*arrays)


def local(frames, cotangent, spatial_weight, temporal_kernel):
    n = lax.axis_size("tm")
    nspan = lax.axis_size("span")
    _, ch, rows, width = frames.shape
    assert rows == n and ch == 64 and width == LANES and frames.shape[0] == 1
    gscale = float(n * rows * nspan * width) ** (-0.5)
    block = (n, ch, LANES)
    pad = (9 * (32 // n) + 7) // 8 * 8

    def vmem(shape, dtype):
        return pltpu.VMEM(shape, dtype)

    spec = pl.BlockSpec(memory_space=pltpu.VMEM)
    results = pl.pallas_call(
        functools.partial(kernel, n, nspan, gscale),
        name="space_time_block",
        out_shape=(
            jax.ShapeDtypeStruct(frames.shape, BF16),
            jax.ShapeDtypeStruct(frames.shape, BF16),
            jax.ShapeDtypeStruct((3, 3, ch, ch), F32),
            jax.ShapeDtypeStruct((n, ch), F32),
        ),
        in_specs=[pl.BlockSpec(memory_space=pltpu.HBM)] * 4,
        out_specs=(spec,) * 4,
        scratch_shapes=[
            vmem(frames.shape, BF16),
            vmem(frames.shape, BF16),
            vmem(spatial_weight.shape, BF16),
            vmem((n, ch), BF16),
            vmem((n * ch, LANES), F32),
            vmem((3 * ch, 3 * ch), BF16),
            vmem((3 * ch, 3 * ch), BF16),
            vmem((n + 2, ch, LANES), BF16),
            vmem((3 * ch, n * LANES), BF16),
            vmem(block, BF16),
            vmem(block, BF16),
            vmem(block, F32),
            vmem(block, F32),
            vmem(block, BF16),
            vmem(block, BF16),
            vmem(block, F32),
            vmem(block, F32),
            vmem(block, F32),
            vmem(block, BF16),
            vmem(block, BF16),
            vmem(block, BF16),
            vmem(block, BF16),
            vmem((n + 2, ch, LANES), BF16),
            vmem((3 * ch, n * LANES), BF16),
            vmem((n * ch, LANES), F32),
            vmem((ch, LANES), F32),
            vmem((nspan, n // 2, LANES), F32),
            vmem((n, n // 2, LANES), F32),
            vmem((n * pad, LANES), F32),
            vmem((n, pad, LANES), F32),
            vmem((pad, LANES), F32),
            vmem((nspan, pad, LANES), F32),
            vmem((pad, LANES), F32),
            vmem((n * pad, LANES), F32),
            pltpu.SemaphoreType.DMA((25,)),
            pltpu.SemaphoreType.DMA((25,)),
            pltpu.SemaphoreType.DMA((4,)),
        ],
        compiler_params=pltpu.CompilerParams(
            collective_id=0, has_side_effects=True, vmem_limit_bytes=50 * 2**20
        ),
    )(
        *[
            pltpu.with_memory_space_constraint(x, pltpu.HBM)
            for x in (frames, cotangent, spatial_weight, temporal_kernel.T)
        ]
    )
    block_output, input_grad, weight_grad, kernel_grad = store(*results)
    return block_output, input_grad, weight_grad, kernel_grad.T


def solution(mesh):
    placed = (P("tm", None, "span", None), P("tm", None, "span", None), P(), P())
    return jax.shard_map(
        local,
        mesh=mesh,
        in_specs=placed,
        out_specs=placed,
        check_vma=False,
    )
```

```python
import functools

import jax
import jax.numpy as jnp
from jax import lax
from jax.experimental import pallas as pl
from jax.experimental.pallas import tpu as pltpu
from jax.sharding import PartitionSpec as P

F32 = jnp.float32
BF16 = jnp.bfloat16
MESH = pl.DeviceIdType.MESH
LANES = 128
BLK = 8


def causal_sums(n, x_at, k_at, put):
    for tb in range(0, n, BLK):
        acc = [None] * BLK
        for rb in range(0, tb + BLK, BLK):
            xs = [x_at(rb + j) for j in range(BLK)]
            ks = {}
            for lag in range(max(0, tb - rb - BLK + 1), tb - rb + BLK):
                ks[lag] = k_at(lag)
            for i in range(BLK):
                for j in range(BLK):
                    lag = tb + i - rb - j
                    if lag >= 0:
                        term = ks[lag] * xs[j]
                        acc[i] = term if acc[i] is None else acc[i] + term
        for i in range(BLK):
            put(tb + i, acc[i])


def lag_sums(n, t_at, r_at, put):
    acc = {}
    for dist in range(0, n, BLK):
        for rb in range(0, n - dist, BLK):
            ts = [t_at(rb + dist + i) for i in range(BLK)]
            rs = [r_at(rb + j) for j in range(BLK)]
            for i in range(BLK):
                for j in range(BLK):
                    lag = dist + i - j
                    if lag >= 0:
                        term = ts[i] * rs[j]
                        acc[lag] = acc[lag] + term if lag in acc else term
        for lag in sorted(acc):
            if lag <= dist:
                put(lag, acc.pop(lag))
    for lag in sorted(acc):
        put(lag, acc.pop(lag))


def kernel(
    n,
    nspan,
    gscale,
    frames_hbm,
    cot_hbm,
    weight_hbm,
    temporal_hbm,
    block_ref,
    input_grad_ref,
    weight_grad_ref,
    kernel_grad_ref,
    frames_ref,
    cot_ref,
    weight_ref,
    temporal_ref,
    tmp,
    wf,
    wb,
    xp,
    x3,
    cot_t,
    act_t,
    gbuf,
    kb,
    rcot,
    ract,
    xf,
    yf,
    outf,
    back_t,
    along_t,
    rback,
    ralong,
    dp,
    db,
    igf,
    kgbuf,
    kz,
    kp,
    red,
    rred,
    part,
    zpart,
    full,
    gathered,
    send_sems,
    recv_sems,
    load_sems,
):
    me = lax.axis_index("tm")
    sp = lax.axis_index("span")
    xy, zh = me // 2, me % 2
    zl, core = sp // 2, sp % 2
    zcount = nspan
    zi = zh * (nspan // 2) + zl
    pi = xy * 2 + core
    ch = 64

    def tm_dev(t):
        return (t, sp)

    def plane_dev(p):
        return ((p // 2) * 2 + zh, zl * 2 + p % 2)

    def z_dev(z):
        return (xy * 2 + z // (nspan // 2), (z % (nspan // 2)) * 2 + core)

    loads = [
        pltpu.make_async_copy(src, dst, load_sems.at[k])
        for k, (src, dst) in enumerate(
            [
                (cot_hbm, cot_ref),
                (frames_hbm, frames_ref),
                (weight_hbm, weight_ref),
                (temporal_hbm, temporal_ref),
            ]
        )
    ]
    for load in loads:
        load.start()

    barrier = pltpu.get_barrier_semaphore()

    def greet(dev):
        pl.semaphore_signal(barrier, inc=1, device_id=dev, device_id_type=MESH)

    @pl.loop(1, n)
    def _(k):
        greet(tm_dev(lax.rem(me + k, n)))

    @pl.loop(0, n // 2)
    def _(k):
        greet(plane_dev(2 * lax.rem(xy + k, n // 2) + 1 - core))

    @pl.loop(1, zcount // 2)
    def _(k):
        greet(z_dev(lax.rem(zi + k, zcount)))
        greet(z_dev(lax.rem(zi + zcount - k, zcount)))

    greet((me, lax.rem(sp + 1, nspan)))
    greet((me, lax.rem(sp + nspan - 1, nspan)))

    lane = lax.broadcasted_iota(jnp.int32, (ch, LANES), 1)

    def right(v):
        return jnp.where(lane == 0, 0.0, pltpu.roll(v, 1, 1))

    def left(v):
        return jnp.where(lane == LANES - 1, 0.0, pltpu.roll(v, LANES - 1, 1))

    def rows_first(src, dst, offset):
        @pl.loop(0, ch, unroll=8)
        def _(c):
            tmp[pl.ds(c, n, stride=ch), :] = src[0, c].astype(F32)

        @pl.loop(0, n, unroll=4)
        def _(r):
            dst[r + offset] = tmp[pl.ds(pl.multiple_of(r * ch, ch), ch), :].astype(BF16)

    loads[0].wait()
    rows_first(cot_ref, cot_t, 0)
    loads[1].wait()
    rows_first(frames_ref, xp, 1)

    @pl.when(sp == 0)
    def _():
        xp[0] = jnp.zeros((ch, LANES), BF16)
        dp[0] = jnp.zeros((ch, LANES), BF16)

    @pl.when(sp == nspan - 1)
    def _():
        xp[n + 1] = jnp.zeros((ch, LANES), BF16)
        dp[n + 1] = jnp.zeros((ch, LANES), BF16)

    def row_cols(s):
        return pl.ds(pl.multiple_of(s * LANES, LANES), LANES)

    def load_taps(s):
        for a in range(3):
            x3[a * ch : (a + 1) * ch, row_cols(s)] = xp[s + a]

    def forward_rows(rows):
        taps = jnp.concatenate([x3[:, row_cols(s)] for s in rows], axis=1)
        out = jnp.dot(wf[...], taps, preferred_element_type=F32)
        for k, s in enumerate(rows):
            o = out[:, k * LANES : (k + 1) * LANES]
            hidden = o[ch : 2 * ch] + right(o[:ch]) + left(o[2 * ch :])
            sigma = jax.nn.sigmoid(hidden)
            act_t[s] = (hidden * sigma).astype(BF16)
            gbuf[s] = sigma * (1.0 + hidden * (1.0 - sigma))

    pl.semaphore_wait(barrier, n - 1 + n // 2 + 2 * (zcount // 2 - 1) + 2)

    def exchange(src, dst, idx, k, lo, size):
        peer = lax.rem(me + k, n)
        return pltpu.make_async_remote_copy(
            src_ref=src.at[peer, pl.ds(lo, size)],
            dst_ref=dst.at[me, pl.ds(lo, size)],
            send_sem=send_sems.at[idx],
            recv_sem=recv_sems.at[idx],
            device_id=tm_dev(peer),
            device_id_type=MESH,
        )

    def start_far(src, dst, idx, lo, size, first, last):
        @pl.loop(first, last)
        def _(k):
            exchange(src, dst, idx, 2 * k + 1, lo, size).start()

    def start_exchange(src, dst, idx, lo=0, size=64, held=0):
        start_far(src, dst, idx, lo, size, 0, n // 2 - held)

        @pl.loop(1, n // 2)
        def _(k):
            exchange(src, dst, idx, 2 * k, lo, size).start()

        dst[me, lo : lo + size] = src[me, lo : lo + size]

    def start_held(src, dst, idx, lo, size, held):
        start_far(src, dst, idx, lo, size, n // 2 - held, n // 2)

    def all_of(buf, idx, lo=0, size=64):
        view = buf.at[pl.ds(0, n - 1), pl.ds(lo, size)]
        return pltpu.make_async_remote_copy(
            src_ref=view,
            dst_ref=view,
            send_sem=send_sems.at[idx],
            recv_sem=recv_sems.at[idx],
            device_id=tm_dev(lax.rem(me + 1, n)),
            device_id_type=MESH,
        )

    def halo(buf, idx):
        up = pltpu.make_async_remote_copy(
            src_ref=buf.at[n],
            dst_ref=buf.at[0],
            send_sem=send_sems.at[idx],
            recv_sem=recv_sems.at[idx],
            device_id=(me, sp + 1),
            device_id_type=MESH,
        )
        down = pltpu.make_async_remote_copy(
            src_ref=buf.at[1],
            dst_ref=buf.at[n + 1],
            send_sem=send_sems.at[idx + 1],
            recv_sem=recv_sems.at[idx + 1],
            device_id=(me, sp - 1),
            device_id_type=MESH,
        )
        return up, down

    def start_halo(buf, idx):
        up, down = halo(buf, idx)

        @pl.when(sp < nspan - 1)
        def _():
            up.start()

        @pl.when(sp > 0)
        def _():
            down.start()

    def finish_halo(buf, idx):
        up, down = halo(buf, idx)

        @pl.when(sp > 0)
        def _():
            up.wait_recv()

        @pl.when(sp < nspan - 1)
        def _():
            down.wait_recv()

        @pl.when(sp < nspan - 1)
        def _():
            up.wait_send()

        @pl.when(sp > 0)
        def _():
            down.wait_send()

    start_halo(xp, 0)
    half = ch // 4
    cot_sems, back_sems, act_sems, along_sems = (4, 15, 17, 18), (6, 16, 19, 20), (5, 11, 21, 22), (7, 12, 23, 24)
    for h in range(4):
        start_exchange(cot_t, rcot, cot_sems[h], h * half, half)

    loads[2].wait()
    loads[3].wait()
    wide = []
    for b in range(3):
        wide.append(jnp.concatenate([weight_ref[a, b].astype(F32) for a in range(3)], axis=1))
    wf[...] = jnp.concatenate(wide, axis=0).astype(BF16)
    wide = []
    for j in range(3):
        wide.append(jnp.concatenate([weight_ref[2 - j, b].astype(F32) for b in range(3)], axis=1))
    wb[...] = jnp.concatenate(wide, axis=0).T.astype(BF16)

    @pl.loop(1, n - 1, unroll=2)
    def _(s):
        load_taps(s)


    @pl.loop(0, (n - 2) // 2, unroll=3)
    def _(p):
        forward_rows([1 + 2 * p, 2 + 2 * p])

    finish_halo(xp, 0)
    load_taps(0)
    load_taps(n - 1)
    forward_rows([0, n - 1])

    columns = temporal_ref[...].astype(F32).T
    for lag in range(n):
        kb[lag] = jnp.broadcast_to(columns[:, lag : lag + 1], (ch, LANES))

    def chan(c):
        return pl.ds(pl.multiple_of(c * 8, 8), 8)

    def back_half(h, in_idx, out_idx):
        lo = h * half
        all_of(rcot, in_idx, lo, half).wait_recv()

        @pl.loop(0, n, unroll=4)
        def _(t):
            yf[t, lo : lo + half] = rcot[t, lo : lo + half].astype(F32)

        @pl.loop(h * (half // 8), (h + 1) * (half // 8))
        def _(c):
            def put(t, v):
                outf[n - 1 - t, chan(c), :] = v

            causal_sums(
                n, lambda t: yf[n - 1 - t, chan(c), :], lambda lag: kb[lag, chan(c), :], put
            )

        @pl.loop(0, n, unroll=4)
        def _(t):
            back_t[t, lo : lo + half] = outf[t, lo : lo + half].astype(BF16)

        start_exchange(back_t, rback, out_idx, lo, half)

    for h in range(4):
        back_half(h, cot_sems[h], back_sems[h])
    for h in range(4):
        start_exchange(act_t, ract, act_sems[h], h * half, half)

    lane8 = lax.broadcasted_iota(jnp.int32, (8, LANES), 1)

    def take_act(h, in_idx):
        lo = h * half
        all_of(ract, in_idx, lo, half).wait_recv()

        @pl.loop(0, n, unroll=4)
        def _(t):
            xf[t, lo : lo + half] = ract[t, lo : lo + half].astype(F32)

    def along_half(h, out_idx, held=0):
        lo = h * half

        @pl.loop(h * (half // 8), (h + 1) * (half // 8))
        def _(c):
            def put(t, v):
                outf[t, chan(c), :] = v

            causal_sums(n, lambda t: xf[t, chan(c), :], lambda lag: kb[lag, chan(c), :], put)

        @pl.loop(0, n, unroll=4)
        def _(t):
            along_t[t, lo : lo + half] = outf[t, lo : lo + half].astype(BF16)

        start_exchange(along_t, ralong, out_idx, lo, half, held=held)

    def lag_half(h):
        @pl.loop(h * (half // 8), (h + 1) * (half // 8))
        def _(c):
            total = [jnp.zeros((8, LANES), F32)]

            def put(lag, v):
                row = jnp.sum(v, axis=1, keepdims=True)
                total[0] = jnp.where(lane8 == lag, row, total[0])

            lag_sums(n, lambda t: yf[t, chan(c), :], lambda r: xf[r, chan(c), :], put)
            kgbuf[chan(c), :] = total[0]

    for h in range(4):
        all_of(rback, back_sems[h], h * half, half).wait_recv()

    def gate_row(s):
        v = rback[s].astype(F32) * gbuf[s]
        dp[s + 1] = v.astype(BF16)
        db[:ch, row_cols(s)] = left(v).astype(BF16)
        db[ch : 2 * ch, row_cols(s)] = v.astype(BF16)
        db[2 * ch :, row_cols(s)] = right(v).astype(BF16)

    gate_row(0)
    gate_row(n - 1)
    start_halo(dp, 2)

    @pl.loop(1, n - 1, unroll=5 if (n - 2) % 5 == 0 else 2)
    def _(s):
        gate_row(s)

    grads = lax.dot_general(
        db[...], x3[...], (((1,), (1,)), ((), ())), preferred_element_type=F32
    )
    per = 32 // n
    used = 9 * per
    pad = (used + 7) // 8 * 8
    for a in range(3):
        for b in range(3):
            tap = grads[b * ch : (b + 1) * ch, a * ch : (a + 1) * ch]
            tap = jnp.concatenate([tap[: ch // 2], tap[ch // 2 :]], axis=1)
            for j in range(per):
                at = (a * 3 + b) * per + j
                red[pl.ds(at, n, stride=pad), :] = tap[j * n : (j + 1) * n]

    def chunk(buf, k):
        return buf.at[pl.ds(pl.multiple_of(k * pad, pad), used)]

    def plane_copy(src, dst, idx, peer):
        return pltpu.make_async_remote_copy(
            src_ref=src,
            dst_ref=dst,
            send_sem=send_sems.at[idx],
            recv_sem=recv_sems.at[idx],
            device_id=plane_dev(peer),
            device_id_type=MESH,
        )

    @pl.loop(1, n)
    def _(k):
        peer = lax.rem(pi + k, n)
        plane_copy(chunk(red, peer), rred.at[pi, pl.ds(0, used)], 8, peer).start()

    rred[pi, 0:used, :] = red[pl.ds(pl.multiple_of(pi * pad, pad), used), :]

    def backward_rows(rows):
        taps = jnp.concatenate(
            [jnp.concatenate([dp[s + j] for j in range(3)], axis=0) for s in rows], axis=1
        )
        out = jnp.dot(wb[...], taps, preferred_element_type=F32)
        for k, s in enumerate(rows):
            o = out[:, k * LANES : (k + 1) * LANES]
            igf[pl.ds(pl.multiple_of(s * ch, ch), ch), :] = (
                o[ch : 2 * ch] + left(o[:ch]) + right(o[2 * ch :])
            )

    for h in range(2):
        take_act(h, act_sems[h])
        along_half(h, along_sems[h])


    def many(buf, count, idx):
        view = buf.at[pl.ds(0, count)]
        return plane_copy(view, view, idx, lax.rem(pi + 1, n))

    def all_chunks(buf, count, idx):
        view = buf.at[pl.ds(0, count), pl.ds(0, used)]
        return plane_copy(view, view, idx, lax.rem(pi + 1, n))

    lag_half(0)
    lag_half(1)
    all_chunks(rred, n - 1, 8).wait_recv()
    part[0:used, :] = jnp.sum(rred[:, 0:used, :], axis=0)

    def z_copy(src, dst, idx, k):
        return pltpu.make_async_remote_copy(
            src_ref=src,
            dst_ref=dst,
            send_sem=send_sems.at[idx],
            recv_sem=recv_sems.at[idx],
            device_id=z_dev(lax.rem(zi + k, zcount)),
            device_id_type=MESH,
        )

    @pl.loop(1, zcount)
    def _(k):
        z_copy(part.at[pl.ds(0, used)], zpart.at[zi, pl.ds(0, used)], 9, k).start()

    zpart[zi, 0:used, :] = part[0:used, :]

    take_act(2, act_sems[2])
    along_half(2, along_sems[2])
    lag_half(2)
    take_act(3, act_sems[3])
    lag_half(3)
    lags = kgbuf[...].T[:n]
    kz[zi] = jnp.concatenate([lags[: n // 2], lags[n // 2 :]], axis=1)

    @pl.loop(1, zcount)
    def _(k):
        z_copy(kz.at[zi], kz.at[zi], 13, k).start()

    along_half(3, along_sems[3], held=n * 8 // 32)


    all_chunks(zpart, zcount - 1, 9).wait_recv()
    full[0:used, :] = jnp.sum(zpart[:, 0:used, :], axis=0) * gscale

    @pl.loop(1, n)
    def _(k):
        peer = lax.rem(pi + k, n)
        plane_copy(full.at[pl.ds(0, used)], chunk(gathered, pi), 10, peer).start()

    gathered[pl.ds(pl.multiple_of(pi * pad, pad), used), :] = full[0:used, :]

    many(kz, zcount - 1, 13).wait_recv()
    kp[pi] = jnp.sum(kz[...], axis=0) * gscale

    @pl.loop(1, n)
    def _(k):
        plane_copy(kp.at[pi], kp.at[pi], 14, lax.rem(pi + k, n)).start()

    start_held(along_t, ralong, along_sems[3], 3 * half, half, n * 8 // 32)

    @pl.loop(0, (n - 2) // 2, unroll=3)
    def _(p):
        backward_rows([1 + 2 * p, 2 + 2 * p])

    finish_halo(dp, 2)
    backward_rows([0, n - 1])

    @pl.loop(0, ch, unroll=8)
    def _(c):
        input_grad_ref[0, c] = (
            cot_ref[0, c].astype(F32) + igf[pl.ds(c, n, stride=ch), :]
        ).astype(BF16)

    def output_half(h, idx):
        lo = h * half
        all_of(ralong, idx, lo, half).wait_recv()

        @pl.loop(0, n, unroll=4)
        def _(r):
            tmp[pl.ds(pl.multiple_of(r * ch + lo, half), half), :] = ralong[
                r, lo : lo + half
            ].astype(F32)

        @pl.loop(lo, lo + half, unroll=8)
        def _(c):
            block_ref[0, c] = (
                frames_ref[0, c].astype(F32) + tmp[pl.ds(c, n, stride=ch), :]
            ).astype(BF16)

    for h in range(3):
        output_half(h, along_sems[h])

    many(kp, n - 1, 14).wait_recv()
    lags = jnp.sum(kp[...], axis=0)
    kernel_grad_ref[...] = jnp.concatenate([lags[:, :ch], lags[:, ch:]], axis=0)

    all_chunks(rred, n - 1, 10).wait_recv()
    for a in range(3):
        for b in range(3):
            rows = []
            for j in range(per):
                at = (a * 3 + b) * per + j
                rows.append(gathered[pl.ds(at, n, stride=pad), :])
            tap = jnp.concatenate(rows, axis=0)
            weight_grad_ref[a, b] = jnp.concatenate([tap[:, :ch], tap[:, ch:]], axis=0)

    output_half(3, along_sems[3])

    for buf, sems in ((rcot, cot_sems), (rback, back_sems), (ract, act_sems), (ralong, along_sems)):
        for h in range(4):
            all_of(buf, sems[h], h * half, half).wait_send()
    many(kz, zcount - 1, 13).wait_send()
    many(kp, n - 1, 14).wait_send()
    all_chunks(rred, n - 1, 8).wait_send()
    all_chunks(zpart, zcount - 1, 9).wait_send()
    all_chunks(rred, n - 1, 10).wait_send()


def store_kernel(*refs):
    count = len(refs) // 2
    sems = refs[-1]
    copies = [
        pltpu.make_async_copy(refs[k], refs[count + k], sems.at[k]) for k in range(count)
    ]
    for copy in copies:
        copy.start()
    for copy in copies:
        copy.wait()


def store(*arrays):
    count = len(arrays)
    return pl.pallas_call(
        store_kernel,
        name="store",
        out_shape=tuple(jax.ShapeDtypeStruct(x.shape, x.dtype) for x in arrays),
        in_specs=[pl.BlockSpec(memory_space=pl.ANY)] * count,
        out_specs=(pl.BlockSpec(memory_space=pl.ANY),) * count,
        scratch_shapes=[pltpu.SemaphoreType.DMA((count,))],
        compiler_params=pltpu.CompilerParams(vmem_limit_bytes=2**20),
    )(*arrays)


def local(frames, cotangent, spatial_weight, temporal_kernel):
    n = lax.axis_size("tm")
    nspan = lax.axis_size("span")
    _, ch, rows, width = frames.shape
    assert rows == n and ch == 64 and width == LANES and frames.shape[0] == 1
    gscale = float(n * rows * nspan * width) ** (-0.5)
    block = (n, ch, LANES)
    pad = (9 * (32 // n) + 7) // 8 * 8

    def vmem(shape, dtype):
        return pltpu.VMEM(shape, dtype)

    spec = pl.BlockSpec(memory_space=pltpu.VMEM)
    results = pl.pallas_call(
        functools.partial(kernel, n, nspan, gscale),
        name="space_time_block",
        out_shape=(
            jax.ShapeDtypeStruct(frames.shape, BF16),
            jax.ShapeDtypeStruct(frames.shape, BF16),
            jax.ShapeDtypeStruct((3, 3, ch, ch), F32),
            jax.ShapeDtypeStruct((n, ch), F32),
        ),
        in_specs=[pl.BlockSpec(memory_space=pltpu.HBM)] * 4,
        out_specs=(spec,) * 4,
        scratch_shapes=[
            vmem(frames.shape, BF16),
            vmem(frames.shape, BF16),
            vmem(spatial_weight.shape, BF16),
            vmem((n, ch), BF16),
            vmem((n * ch, LANES), F32),
            vmem((3 * ch, 3 * ch), BF16),
            vmem((3 * ch, 3 * ch), BF16),
            vmem((n + 2, ch, LANES), BF16),
            vmem((3 * ch, n * LANES), BF16),
            vmem(block, BF16),
            vmem(block, BF16),
            vmem(block, F32),
            vmem(block, F32),
            vmem(block, BF16),
            vmem(block, BF16),
            vmem(block, F32),
            vmem(block, F32),
            vmem(block, F32),
            vmem(block, BF16),
            vmem(block, BF16),
            vmem(block, BF16),
            vmem(block, BF16),
            vmem((n + 2, ch, LANES), BF16),
            vmem((3 * ch, n * LANES), BF16),
            vmem((n * ch, LANES), F32),
            vmem((ch, LANES), F32),
            vmem((nspan, n // 2, LANES), F32),
            vmem((n, n // 2, LANES), F32),
            vmem((n * pad, LANES), F32),
            vmem((n, pad, LANES), F32),
            vmem((pad, LANES), F32),
            vmem((nspan, pad, LANES), F32),
            vmem((pad, LANES), F32),
            vmem((n * pad, LANES), F32),
            pltpu.SemaphoreType.DMA((25,)),
            pltpu.SemaphoreType.DMA((25,)),
            pltpu.SemaphoreType.DMA((4,)),
        ],
        compiler_params=pltpu.CompilerParams(
            collective_id=0, has_side_effects=True, vmem_limit_bytes=50 * 2**20
        ),
    )(
        *[
            pltpu.with_memory_space_constraint(x, pltpu.HBM)
            for x in (frames, cotangent, spatial_weight, temporal_kernel.T)
        ]
    )
    block_output, input_grad, weight_grad, kernel_grad = store(*results)
    return block_output, input_grad, weight_grad, kernel_grad.T


def solution(mesh):
    placed = (P("tm", None, "span", None), P("tm", None, "span", None), P(), P())
    return jax.shard_map(
        local,
        mesh=mesh,
        in_specs=placed,
        out_specs=placed,
        check_vma=False,
    )
```
